32 devices in a mesh: groups: 2 (over y), section: 4 (over z), head: 4 (over x, core).
Axes of the slice: x: 2, y: 2, z: 4, core: 2. Of those that a mesh axis runs over, the one named last changes fastest.
Arguments:
- rising: bfloat16 [8, 128, 1024], P(('groups', 'section')), parts along dimension 0, may hold values from -24 to 24
- falling: bfloat16 [8, 128, 1024], P(('groups', 'section')), parts along dimension 0, may hold values from -6 to 6
- stash: bfloat16 [8, 3, 128, 1024], P(('groups', 'section')), parts along dimension 0, may hold values from -24 to 24
- queue: bfloat16 [12, 128, 1024], P('groups'), parts along dimension 0, may hold values from -24 to 24
- order: int32 [12], P('groups'), parts along dimension 0, may hold values from 0 to 5, each once
- buckets: int32 [128, 128], replicated, may hold values from 0 to 31, as said below
- bias_table: float32 [4, 32, 64], P('section', None, 'head'), may hold values from -3 to 260
- gain: float32 [4, 1024], P('section'), may hold values from 0.1 to 1.9
- w_qkv: bfloat16 [4, 1024, 64, 3, 128], P('section', None, 'head'), may hold values from -0.1875 to 0.1875
- w_out: bfloat16 [4, 64, 128, 1024], P('section', 'head'), may hold values from -0.0625 to 0.0625
Outputs:
- rising_out: bfloat16 [8, 128, 1024], P(('groups', 'section')), parts along dimension 0
- falling_out: bfloat16 [8, 128, 1024], P(('groups', 'section')), parts along dimension 0
- table_grad: float32 [8, 32, 64], P(('groups', 'section'), None, 'head'), parts along dimension 0
The draws below stay inside these ranges and needn't reach their ends.
There are 2 independent parts, one for each index of `groups`. The reference program is written for one: setup_inputs(seed, part) draws one part's arguments, and reference() takes and returns one part's arrays. A program takes and returns all parts, laid end to end along the dimension named above; an argument that names none is the same for every part. Nothing has to cross between parts.
Inputs may be any that keep to these rules, and one draw needn't show every extreme that they name: `order`: a permutation of 0 to 5. T5's bidirectional bucket of the key's position minus the query's, 32 buckets, distances of 128 or more in the outermost; positions rise by 1 to 4 from token to token, with one jump of 128 or more.
All inputs are finite; a program needn't handle non-finite values.
Results may differ from the reference program's by a relative error of at most 0.019.
Values may be sent and summed in bfloat16 or wider, within the bound.
A program may use at most 128 MiB of HBM per device.

```python
import math
import jax
import jax.numpy as jnp
from jax import lax

D = 1024
HEADS = 64
HD = 128
NB = 32
MAX_DIST = 128
TOK = 128
TICKS = 3
QUEUE = 6
SECTIONS = 4


bucket_edges = (12, 16, 23, 32, 46, 64, 91)


def scaled_rows(key, shape):
    keys = jax.random.split(key, 3)
    base = jax.random.normal(keys[0], shape, jnp.float32)
    row_scale = jnp.exp(jax.random.uniform(keys[1], shape[:-1] + (1,), jnp.float32, math.log(0.3), math.log(3.0)))
    col_scale = jnp.exp(jax.random.uniform(keys[2], (shape[-1],), jnp.float32, math.log(0.3), math.log(3.0)))
    return jnp.clip(base * row_scale * col_scale, -24.0, 24.0).astype(jnp.bfloat16)


def draw_rising(key, part):
    return scaled_rows(jax.random.fold_in(key, 101), (SECTIONS, TOK, D))


def draw_stash(key, part):
    return scaled_rows(jax.random.fold_in(key, 202), (SECTIONS, TICKS, TOK, D))


def draw_queue(key, part):
    return scaled_rows(jax.random.fold_in(key, 303), (QUEUE, TOK, D))


def draw_buckets(key, part):
    keys = jax.random.split(jax.random.fold_in(key, 404), 2)
    steps_between = jax.random.randint(keys[0], (TOK,), 1, 5, dtype=jnp.int32)
    jump_at = jax.random.randint(keys[1], (), 1, TOK, dtype=jnp.int32)
    token_ids = jnp.arange(TOK, dtype=jnp.int32)
    steps_between = jnp.where(token_ids == jump_at, steps_between + MAX_DIST, steps_between)
    positions = jnp.cumsum(steps_between).astype(jnp.int32)
    offset = positions[:, None] - positions[None, :]
    distance = jnp.abs(offset)
    half = NB // 2
    exact = half // 2
    far = jnp.full(distance.shape, exact, jnp.int32)
    for edge in bucket_edges:
        far = far + (distance >= edge).astype(jnp.int32)
    within = jnp.where(distance < exact, distance, jnp.minimum(far, half - 1))
    return (jnp.where(offset < 0, half, 0) + within).astype(jnp.int32)


def draw_bias_table(key, part):
    keys = jax.random.split(jax.random.fold_in(key, 505), 1)
    table = jnp.clip(jax.random.normal(keys[0], (SECTIONS, NB, HEADS), jnp.float32), -3.0, 3.0)
    return table.astype(jnp.float32)


def block_scale(rng, shape, cuts, low, high):
    level, own = 1.0, jax.random.fold_in(rng, 6)
    for position, parts in cuts:
        draws = jnp.exp(jax.random.uniform(jax.random.fold_in(own, position), (parts,), jnp.float32, low / len(cuts), high / len(cuts)))
        level = level * jnp.repeat(draws, shape[position] // parts).reshape([-1 if axis == position else 1 for axis in range(len(shape))])
    return level


def centred(stream_key, dims, width, bound, cuts=(), kind=jnp.bfloat16):
    factor_of = block_scale(stream_key, dims, cuts, -0.22, 0.18) if cuts else 1.0
    entries = jax.random.normal(stream_key, dims, jnp.float32) * width * factor_of
    return jnp.minimum(jnp.maximum(entries, -bound), bound).astype(kind)


def setup_inputs(seed: int = 0, part: int = 0) -> dict:
    key_list = jax.random.split(jax.random.key(seed), 11)
    part_keys = jax.random.split(jax.random.fold_in(key_list[10], part), 11)
    rising = draw_rising(jax.random.fold_in(jax.random.fold_in(key_list[10], part), 71), part)
    falling = centred(part_keys[1], (SECTIONS, TOK, D), 1.0, 6.0, ((0, 4),))
    stash = draw_stash(jax.random.fold_in(jax.random.fold_in(key_list[10], part), 71), part)
    queue = draw_queue(jax.random.fold_in(jax.random.fold_in(key_list[10], part), 71), part)
    order = jax.random.permutation(part_keys[4], QUEUE).astype(jnp.int32)
    buckets = draw_buckets(jax.random.fold_in(key_list[10], 71), part)
    bias_table = draw_bias_table(jax.random.fold_in(key_list[10], 71), part)
    gain = jnp.clip(1.0 + 0.18 * jax.random.normal(key_list[7], (SECTIONS, D), jnp.float32), 0.1, 1.9)
    w_qkv = centred(key_list[8], (SECTIONS, D, HEADS, 3, HD), D ** -0.5, 0.1875, ((0, 4), (2, 4)))
    w_out = centred(key_list[9], (SECTIONS, HEADS, HD, D), (HEADS * HD) ** -0.5, 0.0625, ((0, 4), (1, 4)))
    return dict(rising=rising, falling=falling, stash=stash, queue=queue, order=order, buckets=buckets, bias_table=bias_table, gain=gain, w_qkv=w_qkv, w_out=w_out)


EPSILON = 1e-06
CONTRACT_LAST = (((1,), (1,)), ((), ()))

def normalize(inputs, gain_row):
    as_float = inputs.astype(jnp.float32)
    inverse = lax.rsqrt(lax.optimization_barrier(jnp.mean(as_float * as_float, axis=-1, keepdims=True)) + EPSILON)
    return ((as_float * inverse * gain_row).astype(jnp.bfloat16), inverse)

def forward_parts(inputs, gain_row, w_in, biases):
    normed, inverse = normalize(inputs, gain_row)
    qkv = jnp.dot(normed, w_in, preferred_element_type=jnp.float32).astype(jnp.bfloat16)
    qkv = qkv.reshape(inputs.shape[0], HEADS, 3, HD)
    queries = qkv[:, :, 0]
    keys_part = qkv[:, :, 1]
    values_part = qkv[:, :, 2]
    scores = jnp.einsum('ihd,jhd->hij', queries.astype(jnp.float32), keys_part.astype(jnp.float32)) * HD ** (-0.5) + biases
    attention_probs = jax.nn.softmax(scores, axis=-1)
    return (inverse, queries, keys_part, values_part, attention_probs, attention_probs.astype(jnp.bfloat16))

def section_forward(inputs, gain_row, w_in, w_back, biases):
    inverse, queries, keys_part, values_part, attention_probs, probs_half = forward_parts(inputs, gain_row, w_in, biases)
    attended = jnp.einsum('hij,jhd->ihd', probs_half.astype(jnp.float32), values_part.astype(jnp.float32))
    attended = attended.astype(jnp.bfloat16).reshape(inputs.shape[0], HEADS * HD)
    projected = jnp.dot(attended, w_back, preferred_element_type=jnp.float32)
    return (inputs.astype(jnp.float32) + projected).astype(jnp.bfloat16)

def section_backward(inputs, cotangent, gain_row, w_in, w_back, biases):
    inverse, queries, keys_part, values_part, attention_probs, probs_half = forward_parts(inputs, gain_row, w_in, biases)
    tokens = inputs.shape[0]
    grad_attn = lax.dot_general(cotangent, w_back, CONTRACT_LAST, preferred_element_type=jnp.float32)
    grad_attn = grad_attn.astype(jnp.bfloat16).reshape(tokens, HEADS, HD).astype(jnp.float32)
    grad_probs = jnp.einsum('ihd,jhd->hij', grad_attn, values_part.astype(jnp.float32))
    grad_value = jnp.einsum('hij,ihd->jhd', probs_half.astype(jnp.float32), grad_attn).astype(jnp.bfloat16)
    grad_scores = attention_probs * (grad_probs - lax.optimization_barrier(jnp.sum(attention_probs * grad_probs, axis=-1, keepdims=True)))
    scores_half = grad_scores.astype(jnp.bfloat16).astype(jnp.float32)
    grad_query = (jnp.einsum('hij,jhd->ihd', scores_half, keys_part.astype(jnp.float32)) * HD ** (-0.5)).astype(jnp.bfloat16)
    grad_key = (jnp.einsum('hij,ihd->jhd', scores_half, queries.astype(jnp.float32)) * HD ** (-0.5)).astype(jnp.bfloat16)
    stacked = jnp.stack([grad_query, grad_key, grad_value], axis=2).reshape(tokens, HEADS * 3 * HD)
    grad_normed = lax.dot_general(stacked, w_in, CONTRACT_LAST, preferred_element_type=jnp.float32)
    as_float = inputs.astype(jnp.float32)
    weighted = gain_row * grad_normed
    cubed = inverse * inverse * inverse
    result = cotangent.astype(jnp.float32) + inverse * weighted - as_float * cubed * lax.optimization_barrier(jnp.mean(as_float * weighted, axis=-1, keepdims=True))
    return (result.astype(jnp.bfloat16), grad_scores)

def reference(rising, falling, stash, queue, order, buckets, bias_table, gain, w_qkv, w_out):
    hbias = jnp.transpose(bias_table[:, buckets, :], (0, 3, 1, 2))
    w_in_all = w_qkv.reshape(SECTIONS, D, HEADS * 3 * HD)
    w_back_all = w_out.reshape(SECTIONS, HEADS * HD, D)
    upward = rising
    downward = falling
    accum = jnp.zeros((SECTIONS, HEADS, TOK, TOK), jnp.float32)

    def one_section(packed):
        arriving, kept_rows, cotangent, gain_row, w_in, w_back, biases = packed
        lifted = section_forward(arriving, gain_row, w_in, w_back, biases)
        lowered, grad_scores = section_backward(kept_rows, cotangent, gain_row, w_in, w_back, biases)
        return (lifted, lowered, grad_scores)
    out_up = upward
    out_down = downward
    for tick_index in range(TICKS):
        kept = stash[:, tick_index]
        out_up, out_down, grad_scores = lax.map(one_section, (upward, kept, downward, gain, w_in_all, w_back_all, hbias))
        accum = accum + grad_scores
        if tick_index + 1 < TICKS:
            arrival = queue[order[tick_index]]
            upward = jnp.concatenate([arrival[None], out_up[:-1]], axis=0)
            downward = jnp.concatenate([out_down[1:], out_up[-1:]], axis=0)

    def fold_table(section_accum):
        flat = section_accum.reshape(HEADS, TOK * TOK).T
        return jax.ops.segment_sum(flat, buckets.reshape(-1), num_segments=NB)
    table_grad = lax.map(fold_table, accum)
    return (out_up, out_down, table_grad)
```

```python
import functools

import jax
import jax.numpy as jnp
from jax import lax
from jax.experimental import pallas as pl
from jax.experimental.pallas import tpu as pltpu
from jax.sharding import PartitionSpec as P

EPSILON = 1e-06
MESH = pl.DeviceIdType.MESH
NN = (((1,), (0,)), ((), ()))
NT = (((1,), (1,)), ((), ()))
TN = (((0,), (0,)), ((), ()))
BF16 = jnp.bfloat16
F32 = jnp.float32


def mm(a, b, dims):
    return lax.dot_general(a, b, dims, preferred_element_type=F32)


def inverse_rms(x):
    return lax.rsqrt(jnp.mean(x * x, axis=-1, keepdims=True) + EPSILON)


def softmax(scores):
    raised = jnp.exp(scores - jnp.max(scores, axis=-1, keepdims=True))
    return raised * (1.0 / jnp.sum(raised, axis=-1, keepdims=True))


def wave_kernel(
    ticks, pair, head_dim, chips, sections, halves, group,
    order, rising, falling, stash, queue, gain, labels, buckets, w_hbm, wo_hbm,
    moved, table,
    bias, raw, w_sem, wo, wo_sem, wq, wk, wv, aq, ak, av, normed, probs, attended,
    gflat, gq, gk, gv, thin, flat_down, total, sums,
    cur, part, near, away, far, share,
    near_send, near_recv, far_send, far_recv,
    lift_send, lift_recv, gather_send, gather_recv, pass_send, pass_recv,
):
    section = lax.axis_index("section")
    head = lax.axis_index("head")
    chip, core = head // 2, lax.rem(head, 2)
    twin = chip * 2 + (1 - core)
    heads, rows = total.shape[:2]
    lanes = flat_down.shape[2]
    tiles = flat_down.shape[0]
    width = tiles * lanes
    steps = heads // pair
    scale = head_dim ** (-0.5)
    half = width // halves
    weights, acts, grads = (wq, wk, wv), (aq, ak, av), (gq, gk, gv)
    last = ticks - 1

    def peer(k):
        return lax.rem(chip + k, chips)

    def remote(src, dst, send, recv, target):
        return pltpu.make_async_remote_copy(
            src_ref=src, dst_ref=dst, send_sem=send, recv_sem=recv,
            device_id=target, device_id_type=MESH,
        )

    def flat(x):
        return x.astype(F32).reshape(rows, width)

    def cut(j):
        return pl.ds(j * half, half)

    def near_copy(which, t, j, k):
        return remote(
            part.at[which, t, peer(k), 1 - core, :, cut(j)], near.at[which, t, k, :, cut(j)],
            near_send.at[which, t, j, k], near_recv.at[which, t, j, k], {"head": twin},
        )

    def far_copy(which, t, j, k):
        return remote(
            away.at[which, t, k - 1, :, cut(j)], far.at[which, t, k - 1, :, cut(j)],
            far_send.at[which, t, j, k - 1], far_recv.at[which, t, j, k - 1],
            {"head": peer(k) * 2 + core},
        )

    def lift_copy(which, t, j, target):
        return remote(
            share.at[which, t, :, cut(j)], cur.at[which, t + 1, chip, core, :, cut(j)],
            lift_send.at[which, t, j], lift_recv.at[which, t, j], {"section": target},
        )

    def gather_copy(which, t, j, k):
        rows_here = cur.at[which, t + 1, chip, core, :, cut(j)]
        return remote(
            rows_here, rows_here,
            gather_send.at[which, t, j, k - 1], gather_recv.at[which, t, j, k - 1],
            {"head": peer(k) * 2 + core},
        )

    def pass_copy(which, t, j, k):
        rows_here = cur.at[which, t + 1, lax.rem(chip - k + chips, chips), core, :, cut(j)]
        return remote(
            rows_here, rows_here,
            pass_send.at[which, t, j, k], pass_recv.at[which, t, j, k], {"head": twin},
        )

    def begin(which, t, j):
        for k in list(range(1, chips)) + [0]:
            near_copy(which, t, j, k).start()

    def fold(which, t, j):
        for k in range(1, chips):
            near_copy(which, t, j, k).wait_recv()
            away[which, t, k - 1, :, cut(j)] = (
                part[which, t, peer(k), core, :, cut(j)].astype(F32)
                + near[which, t, k, :, cut(j)].astype(F32)
            ).astype(BF16)
            far_copy(which, t, j, k).start()

    def ends(which):
        if which == 0:
            return section < sections - 1, section + 1, section > 0, section - 1
        return section > 0, section - 1, section < sections - 1, section + 1

    def reduced(which, t, j):
        near_copy(which, t, j, 0).wait_recv()
        own = part[which, t, chip, core, :, cut(j)].astype(F32) + near[
            which, t, 0, :, cut(j)
        ].astype(F32)
        for k in range(1, chips):
            far_copy(which, t, j, k).wait_recv()
            own = own + far[which, t, k - 1, :, cut(j)].astype(F32)
        return own

    def hand_on(which, t, j, result):
        sends, target, receives, _ = ends(which)
        if t == last:
            cur[which, t + 1, chip, core, :, cut(j)] = result
            return
        share[which, t, :, cut(j)] = result

        @pl.when(sends)
        def _():
            lift_copy(which, t, j, target).start()

        @pl.when(jnp.logical_not(receives))
        def _():
            if which == 0:
                cur[which, t + 1, chip, core, :, cut(j)] = queue[
                    order[t], chip, core, :, cut(j)
                ]
            else:
                cur[which, t + 1, chip, core, :, cut(j)] = share[0, t, :, cut(j)]

    def finish_up(t, j):
        before = cur[0, t, chip, core, :, cut(j)].astype(F32)
        hand_on(0, t, j, (before + reduced(0, t, j)).astype(BF16))

    def finish_down(t):
        own = jnp.concatenate([reduced(1, t, j) for j in range(halves)], axis=-1)
        before = cur[1, t, chip, core].astype(F32)
        x = stash[t, chip, core].astype(F32)
        inverse = inverse_rms(x)
        cubed = inverse * inverse * inverse
        weighted = gain[...] * own
        result = (
            before
            + inverse * weighted
            - x * cubed * jnp.mean(x * weighted, axis=-1, keepdims=True)
        ).astype(BF16)
        for j in range(halves):
            hand_on(1, t, j, result[:, j * half : (j + 1) * half])

    def spread(which, t, j):
        _, _, receives, source = ends(which)
        if t < last:
            @pl.when(receives)
            def _():
                lift_copy(which, t, j, source).wait_recv()

        for k in range(1, chips):
            gather_copy(which, t, j, k).start()
        pass_copy(which, t, j, 0).start()

    def relay(which, t, j):
        for k in range(1, chips):
            gather_copy(which, t, j, k).wait_recv()
            pass_copy(which, t, j, k).start()

    def settle(which, t):
        sends, target, _, _ = ends(which)
        for j in range(halves):
            for k in range(chips):
                pass_copy(which, t, j, k).wait_recv()
        for j in range(halves):
            for k in range(chips):
                near_copy(which, t, j, k).wait_send()
                pass_copy(which, t, j, k).wait_send()
            for k in range(1, chips):
                far_copy(which, t, j, k).wait_send()
                gather_copy(which, t, j, k).wait_send()
            if t < last:
                @pl.when(sends)
                def _(j=j):
                    lift_copy(which, t, j, target).wait_send()

    def beside(blocks):
        return jnp.concatenate(blocks, axis=1)

    def fetch(c):
        return pltpu.make_async_copy(w_hbm.at[:, c], raw.at[c % 2], w_sem.at[c])

    def relay_weights(c, low, count):
        for n in range(count):
            at = pl.ds(pl.multiple_of((low + n) * group, group), group)
            turned = jnp.swapaxes(raw[c % 2, at], 0, 1)
            for h in range(heads):
                weights[c][h, at] = turned[h]

    def normalize(place, x):
        y = (x * inverse_rms(x) * gain[...]).astype(BF16)
        for b in range(tiles):
            normed[b, place * rows : (place + 1) * rows] = y[:, b * lanes : (b + 1) * lanes]

    def lower(x):
        y = x.astype(BF16)
        for b in range(tiles):
            flat_down[b] = y[:, b * lanes : (b + 1) * lanes]

    def project(c, step, place, count=1):
        at = slice(place * rows, (place + count) * rows)
        result = mm(
            beside([normed[b, at] for b in range(tiles)]),
            beside([weights[c][step * pair + h] for h in range(pair)]),
            NN,
        ).astype(BF16)
        for h in range(pair):
            acts[c][step * pair + h, at] = result[:, h * head_dim : (h + 1) * head_dim]

    def project_pairs(place):
        def run(step, carry):
            project(0, step, place)
            project(1, step, place)
            return carry

        lax.fori_loop(0, steps, run, 0)

    def block(emit):
        pl.when(section >= 0)(emit)

    def act(c, place, n):
        return acts[c][n, place * rows : (place + 1) * rows]

    def score(place, step):
        return [
            mm(act(0, place, n), act(1, place, n), NT) * scale + bias[n]
            for n in range(step * pair, (step + 1) * pair)
        ]

    def hooked(hooks, n):
        for action in hooks.get(n, ()):
            action()

    def blend(t, step, scores):
        for h in range(pair):
            probs16 = softmax(scores[h]).astype(BF16)
            n = step * pair + h
            attended[n] = mm(probs16, act(2, 0, n), NN).astype(BF16)

    def keep(step, scores):
        for h in range(pair):
            probs[step * pair + h] = softmax(scores[h])

    def out(t, hooks, base):
        for j in range(halves):
            each = half // lanes
            right = beside([wo[b] for b in range(j * each, (j + 1) * each)])
            left = beside([attended[n] for n in range(heads)])
            result = mm(left, right, NN).astype(BF16)
            part[0, t, :, :, :, cut(j)] = result.reshape(part.shape[2:5] + (half,))
            begin(0, t, j)
            hooked(hooks, base + j)

    def forward(t, hooks, also=None):
        count = 1 if also is None else 2
        if also is None:
            project_pairs(0)
            hooked(hooks, 0)

        @functools.partial(block)
        def _():
            scores = {n: score(0, n) for n in range(min(2, steps))}
            for step in range(steps):
                project(2, step, 0, count)
                extra = score(also, step) if also is not None else None
                if 2 <= step + 2 < steps:
                    scores[step + 2] = score(0, step + 2)
                blend(t, step, scores.pop(step))
                if extra is not None:
                    keep(step, extra)
                hooked(hooks, 2 + step)
            out(t, hooks, 2 + steps)

    def fill(place, hooks):
        project_pairs(place)
        hooked(hooks, 0)

        @functools.partial(block)
        def _():
            scores = {n: score(place, n) for n in range(min(2, steps))}
            for step in range(steps):
                project(2, step, place)
                if step + 2 < steps:
                    scores[step + 2] = score(place, step + 2)
                keep(step, scores.pop(step))
        hooked(hooks, 1 + steps)

    def backward(t, hooks):
        place = t + 1

        def open_grad(step):
            block = slice(step * pair * head_dim, (step + 1) * pair * head_dim)
            result = mm(
                beside([flat_down[b] for b in range(tiles)]),
                beside([wo[b, block] for b in range(tiles)]),
                NT,
            ).astype(BF16)
            for h in range(pair):
                gflat[step * pair + h] = result[:, h * head_dim : (h + 1) * head_dim]

        def score_grads(step):
            for h in range(pair):
                n = step * pair + h
                g = gflat[n]
                grad_probs = mm(g, act(2, place, n), NT)
                p = probs[n]
                gv[n] = mm(p.astype(BF16), g, TN).astype(BF16)
                grad_scores = p * (
                    grad_probs - jnp.sum(p * grad_probs, axis=-1, keepdims=True)
                )
                thin[step % 2, h] = grad_scores.astype(BF16)
                if t == 0:
                    total[n] = grad_scores
                else:
                    total[n] += grad_scores

        def query_key_grads(step):
            for h in range(pair):
                n = step * pair + h
                small = thin[step % 2, h]
                gq[n] = (mm(small, act(1, place, n), NN) * scale).astype(BF16)
                gk[n] = (mm(small, act(0, place, n), TN) * scale).astype(BF16)

        @functools.partial(block)
        def _():
            open_grad(0)
            for step in range(steps):
                score_grads(step)
                if step + 1 < steps:
                    open_grad(step + 1)
                if step > 0:
                    query_key_grads(step - 1)
                hooked(hooks, step)
            query_key_grads(steps - 1)

        for j in range(halves):
            @functools.partial(block)
            def _(j=j):
                rows_of = slice(j * half, (j + 1) * half)
                back = [
                    mm(
                        beside([grads[c][n] for n in range(heads)]),
                        beside([weights[c][n, rows_of] for n in range(heads)]),
                        NT,
                    )
                    for c in (2, 0, 1)
                ]
                result = (back[0] + back[1] + back[2]).astype(BF16)
                part[1, t, :, :, :, cut(j)] = result.reshape(part.shape[2:5] + (half,))
                begin(1, t, j)
                hooked(hooks, steps + j)

    def tables(low, high):
        def run(b, carry):
            chosen = buckets[...] == b
            sums[b] = jnp.concatenate(
                [
                    jnp.sum(jnp.where(chosen, total[h], 0.0), axis=0, keepdims=True)
                    for h in range(total.shape[0])
                ],
                axis=0,
            )
            return carry

        lax.fori_loop(low, high, run, 0)

    def fetch_out(b):
        return pltpu.make_async_copy(
            wo_hbm.at[:, pl.ds(b * lanes, lanes)], wo.at[b], wo_sem.at[b]
        )

    fetch(0).start()
    fetch(1).start()
    barrier = pltpu.get_barrier_semaphore()
    greeted = [twin] + [peer(k) * 2 + core for k in range(1, chips)]
    for other in greeted:
        pl.semaphore_signal(barrier, inc=1, device_id={"head": other}, device_id_type=MESH)

    @pl.when(section > 0)
    def _():
        pl.semaphore_signal(
            barrier, inc=1, device_id={"section": section - 1}, device_id_type=MESH
        )

    @pl.when(section < sections - 1)
    def _():
        pl.semaphore_signal(
            barrier, inc=1, device_id={"section": section + 1}, device_id_type=MESH
        )

    blank = jnp.zeros((heads, lanes - labels.shape[1]), F32)
    lookup = jnp.concatenate([labels[...], blank], axis=1)
    for n in range(heads):
        bias[n] = jnp.take_along_axis(
            jnp.broadcast_to(lookup[n : n + 1], (rows, lanes)), buckets[...], axis=1
        )
    cur[0, 0] = rising[...]
    cur[1, 0] = falling[...]
    lower(flat(falling[...]))
    normalize(0, flat(rising[...]))
    for t in range(ticks):
        normalize(t + 1, flat(stash[t]))

    blocks = width // group
    fetch(0).wait()

    def first(n, carry):
        relay_weights(0, n * 4, 4)
        return carry

    lax.fori_loop(0, blocks // 4, first, 0)
    fetch(2).start()
    for b in range(tiles):
        fetch_out(b).start()

    for c in (1, 2):
        fetch(c).wait()

        def under(step, carry, c=c):
            project(c - 1, step, 0, 2)
            relay_weights(c, step * (blocks // steps), blocks // steps)
            return carry

        lax.fori_loop(0, steps, under, 0)
    for b in range(tiles):
        fetch_out(b).wait()
    pl.semaphore_wait(
        barrier,
        len(greeted)
        + (section > 0).astype(jnp.int32)
        + (section < sections - 1).astype(jnp.int32),
    )

    def do(function, *args):
        return lambda: function(*args)

    def both(function, which, t):
        return [do(function, which, t, j) for j in range(halves)]

    s = steps
    forward(0, {}, also=1)
    for t in range(ticks):
        backward(t, {
            0: both(fold, 0, t),
            s - 1 if s > 1 else 1: [do(finish_up, t, 0)],
            s: [do(finish_up, t, j) for j in range(1, halves)],
            s + halves - 1: both(spread, 0, t),
        })
        if t < last:
            fill(t + 2, {
                0: both(fold, 1, t),
                1 + s: [do(finish_down, t)] + both(relay, 0, t),
            })
            settle(0, t)
            normalize(0, flat(cur[0, t + 1]))
            forward(t + 1, {
                2: both(spread, 1, t),
                1 + s + halves: both(relay, 1, t),
            })
            settle(1, t)
            lower(flat(cur[1, t + 1]))
    count = sums.shape[0]
    tables(0, count // 5)
    for action in both(fold, 1, last) + both(relay, 0, last):
        action()
    settle(0, last)
    moved[0] = cur[0, ticks]
    tables(count // 5, count * 7 // 10)
    finish_down(last)
    for action in both(spread, 1, last):
        action()
    tables(count * 7 // 10, count)
    table[...] = jnp.sum(sums[...], axis=-1)
    for action in both(relay, 1, last):
        action()
    settle(1, last)
    moved[1] = cur[1, ticks]


def per_device(rising, falling, stash, queue, order, buckets, bias_table, gain, w_qkv, w_out):
    sections = lax.axis_size("section")
    head_count = lax.axis_size("head")
    ticks = stash.shape[1]
    rows, width = rising.shape[1:]
    heads, head_dim = w_qkv.shape[2], w_qkv.shape[4]
    chips, part_rows = head_count // 2, rows // head_count
    pair = next(p for p in (4, 2, 1) if heads % p == 0)
    others = max(chips - 1, 1)
    halves, group, lanes = 2, 16, 128
    flat_heads = heads * head_dim
    w_in = jnp.swapaxes(w_qkv[0], 1, 2)
    w_back = w_out[0].reshape(flat_heads, width)
    split = lambda a: a.reshape(a.shape[:-2] + (chips, 2, part_rows, width))
    vmem = pl.BlockSpec(memory_space=pltpu.VMEM)
    tile = (part_rows, width)
    bf16 = lambda *shape: pltpu.VMEM(shape, BF16)
    f32 = lambda *shape: pltpu.VMEM(shape, F32)
    dma = lambda *shape: pltpu.SemaphoreType.DMA(shape)
    moved, table = pl.pallas_call(
        functools.partial(
            wave_kernel, ticks, pair, head_dim, chips, sections, halves, group
        ),
        in_specs=[pl.BlockSpec(memory_space=pltpu.SMEM)] + [vmem] * 7 + [pl.BlockSpec(memory_space=pl.ANY)] * 2,
        out_specs=[vmem] * 2,
        out_shape=[
            jax.ShapeDtypeStruct((2, chips, 2) + tile, BF16),
            jax.ShapeDtypeStruct((bias_table.shape[1], heads), F32),
        ],
        scratch_shapes=[
            f32(heads, rows, rows),
            bf16(2, width, heads, head_dim),
            dma(3),
            bf16(width // lanes, flat_heads, lanes),
            dma(width // lanes),
            bf16(heads, width, head_dim),
            bf16(heads, width, head_dim),
            bf16(heads, width, head_dim),
            bf16(heads, (ticks + 1) * rows, head_dim),
            bf16(heads, (ticks + 1) * rows, head_dim),
            bf16(heads, (ticks + 1) * rows, head_dim),
            bf16(width // lanes, (ticks + 1) * rows, lanes),
            f32(heads, rows, rows),
            bf16(heads, rows, head_dim),
            bf16(heads, rows, head_dim),
            bf16(heads, rows, head_dim),
            bf16(heads, rows, head_dim),
            bf16(heads, rows, head_dim),
            bf16(2, pair, rows, rows),
            bf16(width // lanes, rows, lanes),
            f32(heads, rows, rows),
            f32(bias_table.shape[1], heads, rows),
            bf16(2, ticks + 1, chips, 2, *tile),
            bf16(2, ticks, chips, 2, *tile),
            bf16(2, ticks, chips, *tile),
            bf16(2, ticks, others, *tile),
            bf16(2, ticks, others, *tile),
            bf16(2, ticks, *tile),
            dma(2, ticks, halves, chips), dma(2, ticks, halves, chips),
            dma(2, ticks, halves, others), dma(2, ticks, halves, others),
            dma(2, ticks, halves), dma(2, ticks, halves),
            dma(2, ticks, halves, others), dma(2, ticks, halves, others),
            dma(2, ticks, halves, chips), dma(2, ticks, halves, chips),
        ],
        compiler_params=pltpu.CompilerParams(
            collective_id=0, has_side_effects=True, vmem_limit_bytes=52 << 20
        ),
    )(
        order, split(rising[0]), split(falling[0]), split(stash[0]), split(queue), gain,
        bias_table[0].T, buckets, w_in, w_back,
    )
    moved = moved.reshape(2, 1, rows, width)
    return (moved[0], moved[1], table[None])


def solution(mesh):
    return jax.shard_map(
        per_device,
        mesh=mesh,
        in_specs=(
            P(("groups", "section"), None, None),
            P(("groups", "section"), None, None),
            P(("groups", "section"), None, None, None),
            P("groups", None, None),
            P("groups"),
            P(),
            P("section", None, "head"),
            P("section", None),
            P("section", None, "head", None, None),
            P("section", "head", None, None),
        ),
        out_specs=(
            P(("groups", "section"), None, None),
            P(("groups", "section"), None, None),
            P(("groups", "section"), None, "head"),
        ),
        check_vma=False,
    )
```

```python
import functools

import jax
import jax.numpy as jnp
from jax import lax
from jax.experimental import pallas as pl
from jax.experimental.pallas import tpu as pltpu
from jax.sharding import PartitionSpec as P

EPSILON = 1e-06
MESH = pl.DeviceIdType.MESH
NN = (((1,), (0,)), ((), ()))
NT = (((1,), (1,)), ((), ()))
TN = (((0,), (0,)), ((), ()))
BF16 = jnp.bfloat16
F32 = jnp.float32


def mm(a, b, dims):
    return lax.dot_general(a, b, dims, preferred_element_type=F32)


def inverse_rms(x):
    return lax.rsqrt(jnp.mean(x * x, axis=-1, keepdims=True) + EPSILON)


def softmax(scores):
    raised = jnp.exp(scores - jnp.max(scores, axis=-1, keepdims=True))
    return raised * (1.0 / jnp.sum(raised, axis=-1, keepdims=True))


def wave_kernel(
    ticks, pair, head_dim, chips, sections, halves, pieces, group,
    order, rising, falling, stash_hbm, queue_hbm, gain_hbm, labels_hbm, buckets_hbm,
    w_hbm, wo_hbm,
    moved, table,
    stash, queue, gain, labels, buckets, in_sem,
    bias, raw, w_sem, wo, wo_sem, wq, wk, wv, aq, ak, av, normed, probs, attended,
    gflat, gq, gk, gv, thin, flat_down, total, sums,
    cur, part, near, share,
    near_send, near_recv,
    lift_send, lift_recv, gather_send, gather_recv, pass_send, pass_recv,
):
    section = lax.axis_index("section")
    head = lax.axis_index("head")
    chip, core = head // 2, lax.rem(head, 2)
    twin = chip * 2 + (1 - core)
    heads, rows = total.shape[:2]
    lanes = flat_down.shape[2]
    tiles = flat_down.shape[0]
    width = tiles * lanes
    steps = heads // pair
    scale = head_dim ** (-0.5)
    half = width // halves
    weights, acts, grads = (wq, wk, wv), (aq, ak, av), (gq, gk, gv)
    last = ticks - 1

    def peer(k):
        return lax.rem(chip + k, chips)

    def remote(src, dst, send, recv, target):
        return pltpu.make_async_remote_copy(
            src_ref=src, dst_ref=dst, send_sem=send, recv_sem=recv,
            device_id=target, device_id_type=MESH,
        )

    def flat(x):
        return x.astype(F32).reshape(rows, width)

    def cut(j):
        return pl.ds(j * half, half)

    others = [(k, e) for k in range(chips) for e in range(2) if k + e > 0]
    others = [pair_ for pair_ in others if pair_[0] > 0] + [(0, 1)]

    def scatter_copy(which, t, p, k, e):
        columns = pl.ds(pieces[which][p][0], pieces[which][p][1])
        side = lax.rem(core + e, 2)
        return remote(
            part.at[which, t, peer(k), side, :, columns], near.at[which, t, k, e, :, columns],
            near_send.at[which, t, p, k, e], near_recv.at[which, t, p, k, e],
            {"head": peer(k) * 2 + side},
        )

    def lift_copy(which, t, j, target):
        return remote(
            share.at[which, t, :, cut(j)], cur.at[which, t + 1, chip, core, :, cut(j)],
            lift_send.at[which, t, j], lift_recv.at[which, t, j], {"section": target},
        )

    def gather_copy(which, t, j, k):
        rows_here = cur.at[which, t + 1, chip, core, :, cut(j)]
        return remote(
            rows_here, rows_here,
            gather_send.at[which, t, j, k - 1], gather_recv.at[which, t, j, k - 1],
            {"head": peer(k) * 2 + core},
        )

    def pass_copy(which, t, j, k):
        rows_here = cur.at[which, t + 1, lax.rem(chip - k + chips, chips), core, :, cut(j)]
        return remote(
            rows_here, rows_here,
            pass_send.at[which, t, j, k], pass_recv.at[which, t, j, k], {"head": twin},
        )

    def begin(which, t, p):
        for k, e in others:
            scatter_copy(which, t, p, k, e).start()

    def ends(which):
        if which == 0:
            return section < sections - 1, section + 1, section > 0, section - 1
        return section > 0, section - 1, section < sections - 1, section + 1

    def reduced(which, t, p):
        columns = pl.ds(pieces[which][p][0], pieces[which][p][1])
        own = part[which, t, chip, core, :, columns].astype(F32)
        for k, e in others[::-1]:
            scatter_copy(which, t, p, k, e).wait_recv()
            own = own + near[which, t, k, e, :, columns].astype(F32)
        return own

    def hand_on(which, t, j, result):
        sends, target, receives, _ = ends(which)
        if t == last:
            cur[which, t + 1, chip, core, :, cut(j)] = result
            return
        share[which, t, :, cut(j)] = result

        @pl.when(sends)
        def _():
            lift_copy(which, t, j, target).start()

        @pl.when(jnp.logical_not(receives))
        def _():
            if which == 0:
                cur[which, t + 1, chip, core, :, cut(j)] = queue[
                    order[t], chip, core, :, cut(j)
                ]
            else:
                cur[which, t + 1, chip, core, :, cut(j)] = share[0, t, :, cut(j)]

    def finish_up(t, j):
        before = cur[0, t, chip, core, :, cut(j)].astype(F32)
        hand_on(0, t, j, (before + reduced(0, t, j)).astype(BF16))

    def finish_down(t):
        own = jnp.concatenate([reduced(1, t, p) for p in range(len(pieces[1]))], axis=-1)
        before = cur[1, t, chip, core].astype(F32)
        x = stash[t, chip, core].astype(F32)
        inverse = inverse_rms(x)
        cubed = inverse * inverse * inverse
        weighted = gain[...] * own
        result = (
            before
            + inverse * weighted
            - x * cubed * jnp.mean(x * weighted, axis=-1, keepdims=True)
        ).astype(BF16)
        for j in range(halves):
            hand_on(1, t, j, result[:, j * half : (j + 1) * half])

    def spread(which, t, j):
        _, _, receives, source = ends(which)
        if t < last:
            @pl.when(receives)
            def _():
                lift_copy(which, t, j, source).wait_recv()

        for k in range(1, chips):
            gather_copy(which, t, j, k).start()
        pass_copy(which, t, j, 0).start()

    def relay(which, t, j):
        for k in range(1, chips):
            gather_copy(which, t, j, k).wait_recv()
            pass_copy(which, t, j, k).start()

    def settle(which, t):
        sends, target, _, _ = ends(which)
        for j in range(halves):
            for k in range(chips):
                pass_copy(which, t, j, k).wait_recv()
        for p in range(len(pieces[which])):
            for k, e in others:
                scatter_copy(which, t, p, k, e).wait_send()
        for j in range(halves):
            for k in range(chips):
                pass_copy(which, t, j, k).wait_send()
            for k in range(1, chips):
                gather_copy(which, t, j, k).wait_send()
            if t < last:
                @pl.when(sends)
                def _(j=j):
                    lift_copy(which, t, j, target).wait_send()

    def beside(blocks):
        return jnp.concatenate(blocks, axis=1)

    def fetch(c):
        return pltpu.make_async_copy(w_hbm.at[:, c], raw.at[c % 2], w_sem.at[c])

    def relay_weights(c, low, count):
        for n in range(count):
            at = pl.ds(pl.multiple_of((low + n) * group, group), group)
            turned = jnp.swapaxes(raw[c % 2, at], 0, 1)
            for h in range(heads):
                weights[c][h, at] = turned[h]

    def normalize(place, x):
        y = (x * inverse_rms(x) * gain[...]).astype(BF16)
        for b in range(tiles):
            normed[b, place * rows : (place + 1) * rows] = y[:, b * lanes : (b + 1) * lanes]

    def lower(x):
        y = x.astype(BF16)
        for b in range(tiles):
            flat_down[b] = y[:, b * lanes : (b + 1) * lanes]

    def project(c, step, place, count=1):
        at = slice(place * rows, (place + count) * rows)
        result = mm(
            beside([normed[b, at] for b in range(tiles)]),
            beside([weights[c][step * pair + h] for h in range(pair)]),
            NN,
        ).astype(BF16)
        for h in range(pair):
            acts[c][step * pair + h, at] = result[:, h * head_dim : (h + 1) * head_dim]

    def project_pairs(place, hooks):
        def run(step, carry):
            project(0, step, place)
            project(1, step, place)
            return carry

        lax.fori_loop(0, steps // 2, run, 0)
        hooked(hooks, "mid")
        lax.fori_loop(steps // 2, steps, run, 0)
        hooked(hooks, "pairs")

    def block(emit):
        pl.when(section >= 0)(emit)

    def act(c, place, n):
        return acts[c][n, place * rows : (place + 1) * rows]

    def score(place, step):
        return [
            mm(act(0, place, n), act(1, place, n), NT) * scale + bias[n]
            for n in range(step * pair, (step + 1) * pair)
        ]

    def hooked(hooks, n):
        for action in hooks.get(n, ()):
            action()

    def blend(t, step, scores):
        for h in range(pair):
            probs16 = softmax(scores[h]).astype(BF16)
            n = step * pair + h
            attended[n] = mm(probs16, act(2, 0, n), NN).astype(BF16)

    def keep(step, scores):
        for h in range(pair):
            probs[step * pair + h] = softmax(scores[h])

    def out(t):
        for j in range(halves):
            each = half // lanes
            right = beside([wo[b] for b in range(j * each, (j + 1) * each)])
            left = beside([attended[n] for n in range(heads)])
            result = mm(left, right, NN).astype(BF16)
            part[0, t, :, :, :, cut(j)] = result.reshape(part.shape[2:5] + (half,))
            begin(0, t, j)

    def forward(t, hooks, also=None):
        count = 1 if also is None else 2
        if also is None:
            project_pairs(0, hooks)

        @functools.partial(block)
        def _():
            scores = {n: score(0, n) for n in range(min(2, steps))}
            for step in range(steps):
                project(2, step, 0, count)
                extra = score(also, step) if also is not None else None
                if 2 <= step + 2 < steps:
                    scores[step + 2] = score(0, step + 2)
                blend(t, step, scores.pop(step))
                if extra is not None:
                    keep(step, extra)
            hooked(hooks, "mixed")
            out(t)
        hooked(hooks, "end")

    def fill(place, hooks):
        project_pairs(place, hooks)

        @functools.partial(block)
        def _():
            scores = {n: score(place, n) for n in range(min(2, steps))}
            for step in range(steps):
                project(2, step, place)
                if step + 2 < steps:
                    scores[step + 2] = score(place, step + 2)
                keep(step, scores.pop(step))
        hooked(hooks, "end")

    def backward(t, hooks):
        place = t + 1

        def open_grad(step):
            block = slice(step * pair * head_dim, (step + 1) * pair * head_dim)
            result = mm(
                beside([flat_down[b] for b in range(tiles)]),
                beside([wo[b, block] for b in range(tiles)]),
                NT,
            ).astype(BF16)
            for h in range(pair):
                gflat[step * pair + h] = result[:, h * head_dim : (h + 1) * head_dim]

        def score_grads(step):
            for h in range(pair):
                n = step * pair + h
                g = gflat[n]
                grad_probs = mm(g, act(2, place, n), NT)
                p = probs[n]
                gv[n] = mm(p.astype(BF16), g, TN).astype(BF16)
                grad_scores = p * (
                    grad_probs - jnp.sum(p * grad_probs, axis=-1, keepdims=True)
                )
                thin[step % 2, h] = grad_scores.astype(BF16)
                if t == 0:
                    total[n] = grad_scores
                else:
                    total[n] += grad_scores

        def query_key_grads(step):
            for h in range(pair):
                n = step * pair + h
                small = thin[step % 2, h]
                gq[n] = (mm(small, act(1, place, n), NN) * scale).astype(BF16)
                gk[n] = (mm(small, act(0, place, n), TN) * scale).astype(BF16)

        @functools.partial(block)
        def _():
            open_grad(0)
            for step in range(steps):
                score_grads(step)
                if step + 1 < steps:
                    open_grad(step + 1)
                if step > 0:
                    query_key_grads(step - 1)
                hooked(hooks, step)
            query_key_grads(steps - 1)
        hooked(hooks, "steps")

        for p, (low, size) in enumerate(pieces[1]):
            @functools.partial(block)
            def _(p=p, low=low, size=size):
                rows_of = slice(low, low + size)
                back = [
                    mm(
                        beside([grads[c][n] for n in range(heads)]),
                        beside([weights[c][n, rows_of] for n in range(heads)]),
                        NT,
                    )
                    for c in (2, 0, 1)
                ]
                result = (back[0] + back[1] + back[2]).astype(BF16)
                part[1, t, :, :, :, pl.ds(low, size)] = result.reshape(
                    part.shape[2:5] + (size,)
                )
                begin(1, t, p)
            hooked(hooks, f"back{p}")

    def tables(low, high):
        def run(b, carry):
            chosen = buckets[...] == b
            sums[b] = jnp.concatenate(
                [
                    jnp.sum(jnp.where(chosen, total[h], 0.0), axis=0, keepdims=True)
                    for h in range(total.shape[0])
                ],
                axis=0,
            )
            return carry

        lax.fori_loop(low, high, run, 0)

    def fetch_out(b):
        return pltpu.make_async_copy(
            wo_hbm.at[:, pl.ds(b * lanes, lanes)], wo.at[b], wo_sem.at[b]
        )

    small = [
        pltpu.make_async_copy(source, target, in_sem.at[n])
        for n, (source, target) in enumerate((
            (labels_hbm, labels), (buckets_hbm, buckets), (gain_hbm, gain),
            (rising, cur.at[0, 0]), (falling, cur.at[1, 0]),
            (stash_hbm, stash), (queue_hbm, queue),
        ))
    ]
    for copy in small[:-1]:
        copy.start()
    fetch(0).start()
    small[-1].start()
    fetch(1).start()
    barrier = pltpu.get_barrier_semaphore()
    greeted = [peer(k) * 2 + lax.rem(core + e, 2) for k, e in others]
    for other in greeted:
        pl.semaphore_signal(barrier, inc=1, device_id={"head": other}, device_id_type=MESH)

    @pl.when(section > 0)
    def _():
        pl.semaphore_signal(
            barrier, inc=1, device_id={"section": section - 1}, device_id_type=MESH
        )

    @pl.when(section < sections - 1)
    def _():
        pl.semaphore_signal(
            barrier, inc=1, device_id={"section": section + 1}, device_id_type=MESH
        )

    small[0].wait()
    small[1].wait()
    blank = jnp.zeros((heads, lanes - labels.shape[1]), F32)
    lookup = jnp.concatenate([labels[...], blank], axis=1)
    for n in range(heads):
        bias[n] = jnp.take_along_axis(
            jnp.broadcast_to(lookup[n : n + 1], (rows, lanes)), buckets[...], axis=1
        )
    for copy in small[2:]:
        copy.wait()
    lower(flat(cur[1, 0]))
    normalize(0, flat(cur[0, 0]))
    for t in range(ticks):
        normalize(t + 1, flat(stash[t]))

    blocks = width // group
    fetch(0).wait()

    def first(n, carry):
        relay_weights(0, n * 4, 4)
        return carry

    lax.fori_loop(0, blocks // 4, first, 0)
    fetch(2).start()
    for b in range(tiles):
        fetch_out(b).start()

    for c in (1, 2):
        fetch(c).wait()

        def under(step, carry, c=c):
            project(c - 1, step, 0, 2)
            relay_weights(c, step * (blocks // steps), blocks // steps)
            return carry

        lax.fori_loop(0, steps, under, 0)
    for b in range(tiles):
        fetch_out(b).wait()
    pl.semaphore_wait(
        barrier,
        len(greeted)
        + (section > 0).astype(jnp.int32)
        + (section < sections - 1).astype(jnp.int32),
    )

    def do(function, *args):
        return lambda: function(*args)

    def both(function, which, t):
        return [do(function, which, t, j) for j in range(halves)]

    forward(0, {}, also=1)
    for t in range(ticks):
        backward(t, {
            max(steps - 2, 0): [do(finish_up, t, 0)],
            "steps": [do(finish_up, t, j) for j in range(1, halves)],
            f"back{len(pieces[1]) - 2}": [do(spread, 0, t, 0)],
            f"back{len(pieces[1]) - 1}": [do(spread, 0, t, j) for j in range(1, halves)],
        })
        if t < last:
            fill(t + 2, {"pairs": [do(finish_down, t)] + both(relay, 0, t)})
            settle(0, t)
            normalize(0, flat(cur[0, t + 1]))
            forward(t + 1, {"mid": both(spread, 1, t), "mixed": both(relay, 1, t)})
            settle(1, t)
            lower(flat(cur[1, t + 1]))
    count = sums.shape[0]
    tables(0, count * 2 // 5)
    finish_down(last)
    for action in both(spread, 1, last) + both(relay, 0, last):
        action()
    settle(0, last)
    moved[0] = cur[0, ticks]
    tables(count * 2 // 5, count * 4 // 5)
    for action in both(relay, 1, last):
        action()
    tables(count * 4 // 5, count)
    table[...] = jnp.sum(sums[...], axis=-1)
    settle(1, last)
    moved[1] = cur[1, ticks]


def per_device(rising, falling, stash, queue, order, buckets, bias_table, gain, w_qkv, w_out):
    sections = lax.axis_size("section")
    head_count = lax.axis_size("head")
    ticks = stash.shape[1]
    rows, width = rising.shape[1:]
    heads, head_dim = w_qkv.shape[2], w_qkv.shape[4]
    chips, part_rows = head_count // 2, rows // head_count
    pair = next(p for p in (4, 2, 1) if heads % p == 0)
    others = max(chips - 1, 1)
    halves, group, lanes = 2, 16, 128
    half, quarter = width // 2, width // 4
    pieces = (
        ((0, half), (half, half)),
        ((0, half), (half, quarter), (half + quarter, quarter)),
    )
    flat_heads = heads * head_dim
    w_in = jnp.swapaxes(w_qkv[0], 1, 2)
    w_back = w_out[0].reshape(flat_heads, width)
    split = lambda a: a.reshape(a.shape[:-2] + (chips, 2, part_rows, width))
    vmem = pl.BlockSpec(memory_space=pltpu.VMEM)
    tile = (part_rows, width)
    bf16 = lambda *shape: pltpu.VMEM(shape, BF16)
    f32 = lambda *shape: pltpu.VMEM(shape, F32)
    dma = lambda *shape: pltpu.SemaphoreType.DMA(shape)
    moved, table = pl.pallas_call(
        functools.partial(
            wave_kernel, ticks, pair, head_dim, chips, sections, halves, pieces, group
        ),
        in_specs=[pl.BlockSpec(memory_space=pltpu.SMEM)] + [pl.BlockSpec(memory_space=pltpu.HBM)] * 9,
        out_specs=[vmem] * 2,
        out_shape=[
            jax.ShapeDtypeStruct((2, chips, 2) + tile, BF16),
            jax.ShapeDtypeStruct((bias_table.shape[1], heads), F32),
        ],
        scratch_shapes=[
            bf16(ticks, chips, 2, *tile),
            bf16(queue.shape[0], chips, 2, *tile),
            f32(1, width),
            f32(heads, bias_table.shape[1]),
            pltpu.VMEM(buckets.shape, jnp.int32),
            dma(7),
            f32(heads, rows, rows),
            bf16(2, width, heads, head_dim),
            dma(3),
            bf16(width // lanes, flat_heads, lanes),
            dma(width // lanes),
            bf16(heads, width, head_dim),
            bf16(heads, width, head_dim),
            bf16(heads, width, head_dim),
            bf16(heads, (ticks + 1) * rows, head_dim),
            bf16(heads, (ticks + 1) * rows, head_dim),
            bf16(heads, (ticks + 1) * rows, head_dim),
            bf16(width // lanes, (ticks + 1) * rows, lanes),
            f32(heads, rows, rows),
            bf16(heads, rows, head_dim),
            bf16(heads, rows, head_dim),
            bf16(heads, rows, head_dim),
            bf16(heads, rows, head_dim),
            bf16(heads, rows, head_dim),
            bf16(2, pair, rows, rows),
            bf16(width // lanes, rows, lanes),
            f32(heads, rows, rows),
            f32(bias_table.shape[1], heads, rows),
            bf16(2, ticks + 1, chips, 2, *tile),
            bf16(2, ticks, chips, 2, *tile),
            bf16(2, ticks, chips, 2, *tile),
            bf16(2, ticks, *tile),
            dma(2, ticks, 3, chips, 2), dma(2, ticks, 3, chips, 2),
            dma(2, ticks, halves), dma(2, ticks, halves),
            dma(2, ticks, halves, others), dma(2, ticks, halves, others),
            dma(2, ticks, halves, chips), dma(2, ticks, halves, chips),
        ],
        compiler_params=pltpu.CompilerParams(
            collective_id=0, has_side_effects=True, vmem_limit_bytes=58 << 20
        ),
    )(
        order, split(rising[0]), split(falling[0]), split(stash[0]), split(queue), gain,
        bias_table[0].T, buckets, w_in, w_back,
    )
    moved = moved.reshape(2, 1, rows, width)
    return (moved[0], moved[1], table[None])


def solution(mesh):
    return jax.shard_map(
        per_device,
        mesh=mesh,
        in_specs=(
            P(("groups", "section"), None, None),
            P(("groups", "section"), None, None),
            P(("groups", "section"), None, None, None),
            P("groups", None, None),
            P("groups"),
            P(),
            P("section", None, "head"),
            P("section", None),
            P("section", None, "head", None, None),
            P("section", "head", None, None),
        ),
        out_specs=(
            P(("groups", "section"), None, None),
            P(("groups", "section"), None, None),
            P(("groups", "section"), None, "head"),
        ),
        check_vma=False,
    )
```

```python
import functools

import jax
import jax.numpy as jnp
from jax import lax
from jax.experimental import pallas as pl
from jax.experimental.pallas import tpu as pltpu
from jax.sharding import PartitionSpec as P

EPSILON = 1e-06
MESH = pl.DeviceIdType.MESH
NN = (((1,), (0,)), ((), ()))
NT = (((1,), (1,)), ((), ()))
TN = (((0,), (0,)), ((), ()))
BF16 = jnp.bfloat16
F32 = jnp.float32


def mm(a, b, dims):
    return lax.dot_general(a, b, dims, preferred_element_type=F32)


def inverse_rms(x):
    return lax.rsqrt(jnp.mean(x * x, axis=-1, keepdims=True) + EPSILON)


def softmax(scores):
    raised = jnp.exp(scores - jnp.max(scores, axis=-1, keepdims=True))
    return raised * (1.0 / jnp.sum(raised, axis=-1, keepdims=True))


def wave_kernel(
    ticks, pair, head_dim, chips, sections, halves, pieces, group,
    order, rising, falling, stash_hbm, queue_hbm, gain_hbm, labels_hbm, buckets_hbm,
    w_hbm, wo_hbm,
    moved, table,
    stash, queue, gain, labels, buckets, in_sem,
    bias, raw, w_sem, wo, wo_sem, wq, wk, wv, aq, ak, av, normed, probs, attended,
    gflat, gq, gk, gv, thin, flat_down, total, sums,
    cur, part, near, far, share,
    near_send, near_recv, far_send, far_recv,
    lift_send, lift_recv, pass_send, pass_recv,
):
    section = lax.axis_index("section")
    head = lax.axis_index("head")
    chip, core = head // 2, lax.rem(head, 2)
    twin = chip * 2 + (1 - core)
    heads, rows = total.shape[:2]
    lanes = flat_down.shape[2]
    tiles = flat_down.shape[0]
    width = tiles * lanes
    steps = heads // pair
    scale = head_dim ** (-0.5)
    half = width // halves
    weights, acts, grads = (wq, wk, wv), (aq, ak, av), (gq, gk, gv)
    last = ticks - 1

    def peer(k):
        return lax.rem(chip + k, chips)

    def remote(src, dst, send, recv, target):
        return pltpu.make_async_remote_copy(
            src_ref=src, dst_ref=dst, send_sem=send, recv_sem=recv,
            device_id=target, device_id_type=MESH,
        )

    def flat(x):
        return x.astype(F32).reshape(rows, width)

    def cut(j):
        return pl.ds(j * half, half)

    def piece(which, p):
        return pl.ds(pieces[which][p][0], pieces[which][p][1])

    def near_copy(which, t, p):
        return remote(
            part.at[which, t, 1 - core, :, piece(which, p)],
            near.at[which, t, :, piece(which, p)],
            near_send.at[which, t, p], near_recv.at[which, t, p], {"head": twin},
        )

    def far_copy(which, t, p, k):
        rows_here = far.at[which, t, chip, :, piece(which, p)]
        return remote(
            rows_here, rows_here,
            far_send.at[which, t, p, k - 1], far_recv.at[which, t, p, k - 1],
            {"head": peer(k) * 2 + core},
        )

    def lift_copy(which, t, j, target):
        return remote(
            share.at[which, t, :, cut(j)], cur.at[which, t + 1, core, :, cut(j)],
            lift_send.at[which, t, j], lift_recv.at[which, t, j], {"section": target},
        )

    def pass_copy(which, t, j):
        rows_here = cur.at[which, t + 1, core, :, cut(j)]
        return remote(
            rows_here, rows_here,
            pass_send.at[which, t, j], pass_recv.at[which, t, j], {"head": twin},
        )

    def begin(which, t, p):
        near_copy(which, t, p).start()

    def fold(which, t, p):
        near_copy(which, t, p).wait_recv()
        far[which, t, chip, :, piece(which, p)] = (
            part[which, t, core, :, piece(which, p)].astype(F32)
            + near[which, t, :, piece(which, p)].astype(F32)
        ).astype(BF16)
        for k in range(1, chips):
            far_copy(which, t, p, k).start()

    def ends(which):
        if which == 0:
            return section < sections - 1, section + 1, section > 0, section - 1
        return section > 0, section - 1, section < sections - 1, section + 1

    def reduced(which, t, p):
        for k in range(1, chips):
            far_copy(which, t, p, k).wait_recv()
        own = far[which, t, 0, :, piece(which, p)].astype(F32)
        for c in range(1, chips):
            own = own + far[which, t, c, :, piece(which, p)].astype(F32)
        return own

    def hand_on(which, t, j, result):
        sends, target, receives, _ = ends(which)
        if t == last:
            cur[which, t + 1, core, :, cut(j)] = result
            return
        share[which, t, :, cut(j)] = result

        @pl.when(sends)
        def _():
            lift_copy(which, t, j, target).start()

        @pl.when(jnp.logical_not(receives))
        def _():
            if which == 0:
                cur[which, t + 1, core, :, cut(j)] = queue[order[t], core, :, cut(j)]
            else:
                cur[which, t + 1, core, :, cut(j)] = share[0, t, :, cut(j)]

    def finish_up(t, j):
        before = cur[0, t, core, :, cut(j)].astype(F32)
        hand_on(0, t, j, (before + reduced(0, t, j)).astype(BF16))

    def finish_down(t):
        own = jnp.concatenate([reduced(1, t, p) for p in range(len(pieces[1]))], axis=-1)
        before = cur[1, t, core].astype(F32)
        x = stash[t, core].astype(F32)
        inverse = inverse_rms(x)
        cubed = inverse * inverse * inverse
        weighted = gain[...] * own
        result = (
            before
            + inverse * weighted
            - x * cubed * jnp.mean(x * weighted, axis=-1, keepdims=True)
        ).astype(BF16)
        for j in range(halves):
            hand_on(1, t, j, result[:, j * half : (j + 1) * half])

    def relay(which, t, j):
        _, _, receives, source = ends(which)
        if t < last:
            @pl.when(receives)
            def _():
                lift_copy(which, t, j, source).wait_recv()

        pass_copy(which, t, j).start()

    def settle(which, t):
        sends, target, _, _ = ends(which)
        for j in range(halves):
            pass_copy(which, t, j).wait_recv()
        for p in range(len(pieces[which])):
            near_copy(which, t, p).wait_send()
            for k in range(1, chips):
                far_copy(which, t, p, k).wait_send()
        for j in range(halves):
            pass_copy(which, t, j).wait_send()
            if t < last:
                @pl.when(sends)
                def _(j=j):
                    lift_copy(which, t, j, target).wait_send()

    def beside(blocks):
        return jnp.concatenate(blocks, axis=1)

    def fetch(c):
        return pltpu.make_async_copy(w_hbm.at[:, c], raw.at[c % 2], w_sem.at[c])

    def relay_weights(c, low, count):
        for n in range(count):
            at = pl.ds(pl.multiple_of((low + n) * group, group), group)
            turned = jnp.swapaxes(raw[c % 2, at], 0, 1)
            for h in range(heads):
                weights[c][h, at] = turned[h]

    def normalize(place, x):
        y = (x * inverse_rms(x) * gain[...]).astype(BF16)
        for b in range(tiles):
            normed[b, place * rows : (place + 1) * rows] = y[:, b * lanes : (b + 1) * lanes]

    def lower(x):
        y = x.astype(BF16)
        for b in range(tiles):
            flat_down[b] = y[:, b * lanes : (b + 1) * lanes]

    def project(c, step, place, count=1):
        at = slice(place * rows, (place + count) * rows)
        result = mm(
            beside([normed[b, at] for b in range(tiles)]),
            beside([weights[c][step * pair + h] for h in range(pair)]),
            NN,
        ).astype(BF16)
        for h in range(pair):
            acts[c][step * pair + h, at] = result[:, h * head_dim : (h + 1) * head_dim]

    def project_pairs(place, hooks):
        def run(step, carry):
            project(0, step, place)
            project(1, step, place)
            return carry

        lax.fori_loop(0, steps // 2, run, 0)
        hooked(hooks, "mid")
        lax.fori_loop(steps // 2, steps, run, 0)
        hooked(hooks, "pairs")

    def block(emit):
        pl.when(section >= 0)(emit)

    def act(c, place, n):
        return acts[c][n, place * rows : (place + 1) * rows]

    def score(place, step):
        return [
            mm(act(0, place, n), act(1, place, n), NT) * scale + bias[n]
            for n in range(step * pair, (step + 1) * pair)
        ]

    def hooked(hooks, n):
        for action in hooks.get(n, ()):
            action()

    def blend(t, step, scores):
        for h in range(pair):
            probs16 = softmax(scores[h]).astype(BF16)
            n = step * pair + h
            attended[n] = mm(probs16, act(2, 0, n), NN).astype(BF16)

    def keep(step, scores):
        for h in range(pair):
            probs[step * pair + h] = softmax(scores[h])

    def out(t):
        for j in range(halves):
            each = half // lanes
            right = beside([wo[b] for b in range(j * each, (j + 1) * each)])
            left = beside([attended[n] for n in range(heads)])
            result = mm(left, right, NN).astype(BF16)
            part[0, t, :, :, cut(j)] = result.reshape(part.shape[2:4] + (half,))
            begin(0, t, j)

    def forward(t, hooks, also=None):
        count = 1 if also is None else 2
        if also is None:
            project_pairs(0, hooks)

        @functools.partial(block)
        def _():
            scores = {n: score(0, n) for n in range(min(2, steps))}
            for step in range(steps):
                project(2, step, 0, count)
                extra = score(also, step) if also is not None else None
                if 2 <= step + 2 < steps:
                    scores[step + 2] = score(0, step + 2)
                blend(t, step, scores.pop(step))
                if extra is not None:
                    keep(step, extra)
                hooked(hooks, step)
            out(t)
        hooked(hooks, "end")

    def fill(place, hooks):
        project_pairs(place, hooks)

        @functools.partial(block)
        def _():
            scores = {n: score(place, n) for n in range(min(2, steps))}
            for step in range(steps):
                project(2, step, place)
                if step + 2 < steps:
                    scores[step + 2] = score(place, step + 2)
                keep(step, scores.pop(step))
                hooked(hooks, step)
        hooked(hooks, "end")

    def backward(t, hooks):
        place = t + 1

        def open_grad(step):
            block = slice(step * pair * head_dim, (step + 1) * pair * head_dim)
            result = mm(
                beside([flat_down[b] for b in range(tiles)]),
                beside([wo[b, block] for b in range(tiles)]),
                NT,
            ).astype(BF16)
            for h in range(pair):
                gflat[step * pair + h] = result[:, h * head_dim : (h + 1) * head_dim]

        def score_grads(step):
            for h in range(pair):
                n = step * pair + h
                g = gflat[n]
                grad_probs = mm(g, act(2, place, n), NT)
                p = probs[n]
                gv[n] = mm(p.astype(BF16), g, TN).astype(BF16)
                grad_scores = p * (
                    grad_probs - jnp.sum(p * grad_probs, axis=-1, keepdims=True)
                )
                thin[step % 2, h] = grad_scores.astype(BF16)
                if t == 0:
                    total[n] = grad_scores
                else:
                    total[n] += grad_scores

        def query_key_grads(step):
            for h in range(pair):
                n = step * pair + h
                small = thin[step % 2, h]
                gq[n] = (mm(small, act(1, place, n), NN) * scale).astype(BF16)
                gk[n] = (mm(small, act(0, place, n), TN) * scale).astype(BF16)

        @functools.partial(block)
        def _():
            open_grad(0)
            for step in range(steps):
                score_grads(step)
                if step + 1 < steps:
                    open_grad(step + 1)
                if step > 0:
                    query_key_grads(step - 1)
                hooked(hooks, step)
            query_key_grads(steps - 1)
        hooked(hooks, "steps")

        for p, (low, size) in enumerate(pieces[1]):
            @functools.partial(block)
            def _(p=p, low=low, size=size):
                rows_of = slice(low, low + size)
                back = []
                for c in (2, 0, 1):
                    back.append(mm(
                        beside([grads[c][n] for n in range(heads)]),
                        beside([weights[c][n, rows_of] for n in range(heads)]),
                        NT,
                    ))
                result = (back[0] + back[1] + back[2]).astype(BF16)
                part[1, t, :, :, pl.ds(low, size)] = result.reshape(
                    part.shape[2:4] + (size,)
                )
                begin(1, t, p)
            hooked(hooks, f"back{p}")

    def tables(low, high):
        def run(b, carry):
            chosen = buckets[...] == b
            sums[b] = jnp.concatenate(
                [
                    jnp.sum(jnp.where(chosen, total[h], 0.0), axis=0, keepdims=True)
                    for h in range(total.shape[0])
                ],
                axis=0,
            )
            return carry

        lax.fori_loop(low, high, run, 0)

    def fetch_out(b):
        return pltpu.make_async_copy(
            wo_hbm.at[:, pl.ds(b * lanes, lanes)], wo.at[b], wo_sem.at[b]
        )

    small = [
        pltpu.make_async_copy(source, target, in_sem.at[n])
        for n, (source, target) in enumerate((
            (labels_hbm, labels), (buckets_hbm, buckets), (gain_hbm, gain),
            (rising, cur.at[0, 0]), (falling, cur.at[1, 0]),
            (stash_hbm, stash), (queue_hbm, queue),
        ))
    ]
    for copy in small[:-1]:
        copy.start()
    fetch(0).start()
    small[-1].start()
    fetch(1).start()
    barrier = pltpu.get_barrier_semaphore()
    greeted = [twin] + [peer(k) * 2 + core for k in range(1, chips)]
    for other in greeted:
        pl.semaphore_signal(barrier, inc=1, device_id={"head": other}, device_id_type=MESH)

    @pl.when(section > 0)
    def _():
        pl.semaphore_signal(
            barrier, inc=1, device_id={"section": section - 1}, device_id_type=MESH
        )

    @pl.when(section < sections - 1)
    def _():
        pl.semaphore_signal(
            barrier, inc=1, device_id={"section": section + 1}, device_id_type=MESH
        )

    small[0].wait()
    small[1].wait()
    blank = jnp.zeros((heads, lanes - labels.shape[1]), F32)
    lookup = jnp.concatenate([labels[...], blank], axis=1)
    for n in range(heads):
        bias[n] = jnp.take_along_axis(
            jnp.broadcast_to(lookup[n : n + 1], (rows, lanes)), buckets[...], axis=1
        )
    for copy in small[2:]:
        copy.wait()
    lower(flat(cur[1, 0]))
    normalize(0, flat(cur[0, 0]))
    for t in range(ticks):
        normalize(t + 1, flat(stash[t]))

    blocks = width // group
    fetch(0).wait()

    def first(n, carry):
        relay_weights(0, n * 4, 4)
        return carry

    lax.fori_loop(0, blocks // 4, first, 0)
    fetch(2).start()
    for b in range(tiles):
        fetch_out(b).start()

    for c in (1, 2):
        fetch(c).wait()

        def under(step, carry, c=c):
            project(c - 1, step, 0, 2)
            relay_weights(c, step * (blocks // steps), blocks // steps)
            return carry

        lax.fori_loop(0, steps, under, 0)
    for b in range(tiles):
        fetch_out(b).wait()
    pl.semaphore_wait(
        barrier,
        len(greeted)
        + (section > 0).astype(jnp.int32)
        + (section < sections - 1).astype(jnp.int32),
    )

    def do(function, *args):
        return lambda: function(*args)

    def both(function, which, t):
        return [do(function, which, t, j) for j in range(halves)]

    forward(0, {}, also=1)
    for t in range(ticks):
        down = range(len(pieces[1]))
        backward(t, {
            0: both(fold, 0, t),
            "steps": [do(finish_up, t, 0)],
            "back0": [do(finish_up, t, j) for j in range(1, halves)],
            f"back{down[-2]}": [do(fold, 1, t, p) for p in down[:-2]],
            f"back{down[-1]}": [do(fold, 1, t, p) for p in down[-2:-1]] + [do(relay, 0, t, 0)],
        })
        if t < last:
            final = do(fold, 1, t, down[-1])
            others = [do(relay, 0, t, j) for j in range(1, halves)]
            middle = min(1, steps - 1)
            fill(t + 2, {
                "mid": [final], "pairs": others, max(steps - 2, 0): [do(finish_down, t)],
            })
            settle(0, t)
            normalize(0, flat(cur[0, t + 1]))
            forward(t + 1, {
                "pairs": [do(relay, 1, t, 0)],
                middle: [do(relay, 1, t, j) for j in range(1, halves)],
            })
            settle(1, t)
            lower(flat(cur[1, t + 1]))
    count = sums.shape[0]
    tables(0, count // 5)
    fold(1, last, len(pieces[1]) - 1)
    for j in range(1, halves):
        relay(0, last, j)
    tables(count // 5, count * 3 // 5)
    settle(0, last)
    moved[0] = cur[0, ticks]
    finish_down(last)
    for j in range(halves):
        relay(1, last, j)
    tables(count * 3 // 5, count)
    table[...] = jnp.sum(sums[...], axis=-1)
    settle(1, last)
    moved[1] = cur[1, ticks]


def per_device(rising, falling, stash, queue, order, buckets, bias_table, gain, w_qkv, w_out):
    sections = lax.axis_size("section")
    head_count = lax.axis_size("head")
    ticks = stash.shape[1]
    rows, width = rising.shape[1:]
    heads, head_dim = w_qkv.shape[2], w_qkv.shape[4]
    chips = head_count // 2
    pair = next(p for p in (4, 2, 1) if heads % p == 0)
    others = max(chips - 1, 1)
    halves, group, lanes = 2, 16, 128
    half, quarter = width // 2, width // 4
    pieces = (
        ((0, half), (half, half)),
        ((0, half), (half, quarter), (half + quarter, quarter)),
    )
    flat_heads = heads * head_dim
    w_in = jnp.swapaxes(w_qkv[0], 1, 2)
    w_back = w_out[0].reshape(flat_heads, width)
    split = lambda a: a.reshape(a.shape[:-2] + (2, rows // 2, width))
    vmem = pl.BlockSpec(memory_space=pltpu.VMEM)
    tile = (rows // 2, width)
    bf16 = lambda *shape: pltpu.VMEM(shape, BF16)
    f32 = lambda *shape: pltpu.VMEM(shape, F32)
    dma = lambda *shape: pltpu.SemaphoreType.DMA(shape)
    moved, table = pl.pallas_call(
        functools.partial(
            wave_kernel, ticks, pair, head_dim, chips, sections, halves, pieces, group
        ),
        in_specs=[pl.BlockSpec(memory_space=pltpu.SMEM)] + [pl.BlockSpec(memory_space=pltpu.HBM)] * 9,
        out_specs=[vmem] * 2,
        out_shape=[
            jax.ShapeDtypeStruct((2, 2) + tile, BF16),
            jax.ShapeDtypeStruct((bias_table.shape[1], heads), F32),
        ],
        scratch_shapes=[
            bf16(ticks, 2, *tile),
            bf16(queue.shape[0], 2, *tile),
            f32(1, width),
            f32(heads, bias_table.shape[1]),
            pltpu.VMEM(buckets.shape, jnp.int32),
            dma(7),
            f32(heads, rows, rows),
            bf16(2, width, heads, head_dim),
            dma(3),
            bf16(width // lanes, flat_heads, lanes),
            dma(width // lanes),
            bf16(heads, width, head_dim),
            bf16(heads, width, head_dim),
            bf16(heads, width, head_dim),
            bf16(heads, (ticks + 1) * rows, head_dim),
            bf16(heads, (ticks + 1) * rows, head_dim),
            bf16(heads, (ticks + 1) * rows, head_dim),
            bf16(width // lanes, (ticks + 1) * rows, lanes),
            f32(heads, rows, rows),
            bf16(heads, rows, head_dim),
            bf16(heads, rows, head_dim),
            bf16(heads, rows, head_dim),
            bf16(heads, rows, head_dim),
            bf16(heads, rows, head_dim),
            bf16(2, pair, rows, rows),
            bf16(width // lanes, rows, lanes),
            f32(heads, rows, rows),
            f32(bias_table.shape[1], heads, rows),
            bf16(2, ticks + 1, 2, *tile),
            bf16(2, ticks, 2, *tile),
            bf16(2, ticks, *tile),
            bf16(2, ticks, chips, *tile),
            bf16(2, ticks, *tile),
            dma(2, ticks, 3), dma(2, ticks, 3),
            dma(2, ticks, 3, others), dma(2, ticks, 3, others),
            dma(2, ticks, halves), dma(2, ticks, halves),
            dma(2, ticks, halves), dma(2, ticks, halves),
        ],
        compiler_params=pltpu.CompilerParams(
            collective_id=0, has_side_effects=True, vmem_limit_bytes=54 << 20
        ),
    )(
        order, split(rising[0]), split(falling[0]), split(stash[0]), split(queue), gain,
        bias_table[0].T, buckets, w_in, w_back,
    )
    moved = moved.reshape(2, 1, rows, width)
    return (moved[0], moved[1], table[None])


def solution(mesh):
    return jax.shard_map(
        per_device,
        mesh=mesh,
        in_specs=(
            P(("groups", "section"), None, None),
            P(("groups", "section"), None, None),
            P(("groups", "section"), None, None, None),
            P("groups", None, None),
            P("groups"),
            P(),
            P("section", None, "head"),
            P("section", None),
            P("section", None, "head", None, None),
            P("section", "head", None, None),
        ),
        out_specs=(
            P(("groups", "section"), None, None),
            P(("groups", "section"), None, None),
            P(("groups", "section"), None, "head"),
        ),
        check_vma=False,
    )
```

```python
import functools

import jax
import jax.numpy as jnp
from jax import lax
from jax.experimental import pallas as pl
from jax.experimental.pallas import tpu as pltpu
from jax.sharding import PartitionSpec as P

EPSILON = 1e-06
MESH = pl.DeviceIdType.MESH
NN = (((1,), (0,)), ((), ()))
NT = (((1,), (1,)), ((), ()))
TN = (((0,), (0,)), ((), ()))
BF16 = jnp.bfloat16
F32 = jnp.float32


def mm(a, b, dims):
    return lax.dot_general(a, b, dims, preferred_element_type=F32)


def inverse_rms(x):
    return lax.rsqrt(jnp.mean(x * x, axis=-1, keepdims=True) + EPSILON)


def softmax(scores):
    raised = jnp.exp(scores - jnp.max(scores, axis=-1, keepdims=True))
    return raised * (1.0 / jnp.sum(raised, axis=-1, keepdims=True))


def wave_kernel(
    ticks, pair, head_dim, chips, sections, halves, pieces, group,
    order, rising, falling, stash_hbm, queue_hbm, gain_hbm, labels_hbm, buckets_hbm,
    w_hbm, wo_hbm,
    moved, table,
    stash, queue, gain, labels, buckets, in_sem,
    bias, raw, w_sem, wo, wo_sem, wq, wk, wv, aq, ak, av, normed, probs, attended,
    gflat, gq, gk, gv, thin, flat_down, total, sums,
    cur, part, near, far, share,
    near_send, near_recv, far_send, far_recv,
    lift_send, lift_recv, pass_send, pass_recv,
):
    section = lax.axis_index("section")
    head = lax.axis_index("head")
    chip, core = head // 2, lax.rem(head, 2)
    twin = chip * 2 + (1 - core)
    heads, rows = total.shape[:2]
    lanes = flat_down.shape[2]
    tiles = flat_down.shape[0]
    width = tiles * lanes
    steps = heads // pair
    scale = head_dim ** (-0.5)
    half = width // halves
    weights, acts, grads = (wq, wk, wv), (aq, ak, av), (gq, gk, gv)
    last = ticks - 1

    def peer(k):
        return lax.rem(chip + k, chips)

    def remote(src, dst, send, recv, target):
        return pltpu.make_async_remote_copy(
            src_ref=src, dst_ref=dst, send_sem=send, recv_sem=recv,
            device_id=target, device_id_type=MESH,
        )

    def flat(x):
        return x.astype(F32).reshape(rows, width)

    def cut(j):
        return pl.ds(j * half, half)

    def piece(which, p):
        return pl.ds(pieces[which][p][0], pieces[which][p][1])

    def near_copy(which, t, p):
        return remote(
            part.at[which, t, 1 - core, :, piece(which, p)],
            near.at[which, t, :, piece(which, p)],
            near_send.at[which, t, p], near_recv.at[which, t, p], {"head": twin},
        )

    def far_copy(which, t, p, k):
        rows_here = far.at[which, t, chip, :, piece(which, p)]
        return remote(
            rows_here, rows_here,
            far_send.at[which, t, p, k - 1], far_recv.at[which, t, p, k - 1],
            {"head": peer(k) * 2 + core},
        )

    def lift_copy(which, t, j, target):
        return remote(
            share.at[which, t, :, cut(j)], cur.at[which, t + 1, core, :, cut(j)],
            lift_send.at[which, t, j], lift_recv.at[which, t, j], {"section": target},
        )

    def pass_copy(which, t, j):
        rows_here = cur.at[which, t + 1, core, :, cut(j)]
        return remote(
            rows_here, rows_here,
            pass_send.at[which, t, j], pass_recv.at[which, t, j], {"head": twin},
        )

    def begin(which, t, p):
        near_copy(which, t, p).start()

    def fold(which, t, p):
        near_copy(which, t, p).wait_recv()
        far[which, t, chip, :, piece(which, p)] = (
            part[which, t, core, :, piece(which, p)].astype(F32)
            + near[which, t, :, piece(which, p)].astype(F32)
        ).astype(BF16)
        for k in range(1, chips):
            far_copy(which, t, p, k).start()

    def ends(which):
        if which == 0:
            return section < sections - 1, section + 1, section > 0, section - 1
        return section > 0, section - 1, section < sections - 1, section + 1

    def reduced(which, t, p):
        for k in range(1, chips):
            far_copy(which, t, p, k).wait_recv()
        own = far[which, t, 0, :, piece(which, p)].astype(F32)
        for c in range(1, chips):
            own = own + far[which, t, c, :, piece(which, p)].astype(F32)
        return own

    def hand_on(which, t, j, result):
        sends, target, receives, _ = ends(which)
        if t == last:
            cur[which, t + 1, core, :, cut(j)] = result
            return
        share[which, t, :, cut(j)] = result

        @pl.when(sends)
        def _():
            lift_copy(which, t, j, target).start()

        @pl.when(jnp.logical_not(receives))
        def _():
            if which == 0:
                cur[which, t + 1, core, :, cut(j)] = queue[order[t], core, :, cut(j)]
            else:
                cur[which, t + 1, core, :, cut(j)] = share[0, t, :, cut(j)]

    def finish_up(t, j):
        before = cur[0, t, core, :, cut(j)].astype(F32)
        hand_on(0, t, j, (before + reduced(0, t, j)).astype(BF16))

    def finish_down(t):
        own = jnp.concatenate([reduced(1, t, p) for p in range(len(pieces[1]))], axis=-1)
        before = cur[1, t, core].astype(F32)
        x = stash[t, core].astype(F32)
        inverse = inverse_rms(x)
        cubed = inverse * inverse * inverse
        weighted = gain[...] * own
        result = (
            before
            + inverse * weighted
            - x * cubed * jnp.mean(x * weighted, axis=-1, keepdims=True)
        ).astype(BF16)
        for j in range(halves):
            hand_on(1, t, j, result[:, j * half : (j + 1) * half])

    def relay(which, t, j):
        _, _, receives, source = ends(which)
        if t < last:
            @pl.when(receives)
            def _():
                lift_copy(which, t, j, source).wait_recv()

        pass_copy(which, t, j).start()

    def settle(which, t):
        sends, target, _, _ = ends(which)
        for j in range(halves):
            pass_copy(which, t, j).wait_recv()
        for p in range(len(pieces[which])):
            near_copy(which, t, p).wait_send()
            for k in range(1, chips):
                far_copy(which, t, p, k).wait_send()
        for j in range(halves):
            pass_copy(which, t, j).wait_send()
            if t < last:
                @pl.when(sends)
                def _(j=j):
                    lift_copy(which, t, j, target).wait_send()

    def beside(blocks):
        return jnp.concatenate(blocks, axis=1)

    def fetch(c):
        return pltpu.make_async_copy(w_hbm.at[:, c], raw.at[c % 2], w_sem.at[c])

    def relay_weights(c, low, count):
        for n in range(count):
            at = pl.ds(pl.multiple_of((low + n) * group, group), group)
            turned = jnp.swapaxes(raw[c % 2, at], 0, 1)
            for h in range(heads):
                weights[c][h, at] = turned[h]

    def normalize(place, x):
        y = (x * inverse_rms(x) * gain[...]).astype(BF16)
        for b in range(tiles):
            normed[b, place * rows : (place + 1) * rows] = y[:, b * lanes : (b + 1) * lanes]

    def lower(x):
        y = x.astype(BF16)
        for b in range(tiles):
            flat_down[b] = y[:, b * lanes : (b + 1) * lanes]

    def project(c, step, place, count=1):
        at = slice(place * rows, (place + count) * rows)
        result = mm(
            beside([normed[b, at] for b in range(tiles)]),
            beside([weights[c][step * pair + h] for h in range(pair)]),
            NN,
        ).astype(BF16)
        for h in range(pair):
            acts[c][step * pair + h, at] = result[:, h * head_dim : (h + 1) * head_dim]

    def project_pairs(place, hooks):
        for step in range(steps):
            if step == steps // 2:
                hooked(hooks, "mid")
            project(0, step, place)
            project(1, step, place)
        hooked(hooks, "pairs")

    def block(emit):
        pl.when(section >= 0)(emit)

    def act(c, place, n):
        return acts[c][n, place * rows : (place + 1) * rows]

    def score(place, step):
        return [
            mm(act(0, place, n), act(1, place, n), NT) * scale + bias[n]
            for n in range(step * pair, (step + 1) * pair)
        ]

    def hooked(hooks, n):
        for action in hooks.get(n, ()):
            action()

    def blend(t, step, scores):
        for h in range(pair):
            probs16 = softmax(scores[h]).astype(BF16)
            n = step * pair + h
            attended[n] = mm(probs16, act(2, 0, n), NN).astype(BF16)

    def keep(step, scores):
        for h in range(pair):
            probs[step * pair + h] = softmax(scores[h])

    def out(t):
        for j in range(halves):
            each = half // lanes
            right = beside([wo[b] for b in range(j * each, (j + 1) * each)])
            left = beside([attended[n] for n in range(heads)])
            result = mm(left, right, NN).astype(BF16)
            part[0, t, :, :, cut(j)] = result.reshape(part.shape[2:4] + (half,))
            begin(0, t, j)

    def forward(t, hooks, also=None):
        count = 1 if also is None else 2
        if also is None:
            project_pairs(0, hooks)

        @functools.partial(block)
        def _():
            scores = {n: score(0, n) for n in range(min(2, steps))}
            for step in range(steps):
                project(2, step, 0, count)
                extra = score(also, step) if also is not None else None
                if 2 <= step + 2 < steps:
                    scores[step + 2] = score(0, step + 2)
                blend(t, step, scores.pop(step))
                if extra is not None:
                    keep(step, extra)
                hooked(hooks, step)
            out(t)
        hooked(hooks, "end")

    def fill(place, hooks):
        project_pairs(place, hooks)

        @functools.partial(block)
        def _():
            scores = {n: score(place, n) for n in range(min(2, steps))}
            for step in range(steps):
                project(2, step, place)
                if step + 2 < steps:
                    scores[step + 2] = score(place, step + 2)
                keep(step, scores.pop(step))
                hooked(hooks, step)
        hooked(hooks, "end")

    def backward(t, hooks):
        place = t + 1

        def open_grad(step):
            block = slice(step * pair * head_dim, (step + 1) * pair * head_dim)
            result = mm(
                beside([flat_down[b] for b in range(tiles)]),
                beside([wo[b, block] for b in range(tiles)]),
                NT,
            ).astype(BF16)
            for h in range(pair):
                gflat[step * pair + h] = result[:, h * head_dim : (h + 1) * head_dim]

        def score_grads(step):
            for h in range(pair):
                n = step * pair + h
                g = gflat[n]
                grad_probs = mm(g, act(2, place, n), NT)
                p = probs[n]
                gv[n] = mm(p.astype(BF16), g, TN).astype(BF16)
                grad_scores = p * (
                    grad_probs - jnp.sum(p * grad_probs, axis=-1, keepdims=True)
                )
                thin[step % 2, h] = grad_scores.astype(BF16)
                if t == 0:
                    total[n] = grad_scores
                else:
                    total[n] += grad_scores

        def query_key_grads(step):
            for h in range(pair):
                n = step * pair + h
                small = thin[step % 2, h]
                gq[n] = (mm(small, act(1, place, n), NN) * scale).astype(BF16)
                gk[n] = (mm(small, act(0, place, n), TN) * scale).astype(BF16)

        @functools.partial(block)
        def _():
            open_grad(0)
            for step in range(steps):
                score_grads(step)
                if step + 1 < steps:
                    open_grad(step + 1)
                if step > 0:
                    query_key_grads(step - 1)
                hooked(hooks, step)
            query_key_grads(steps - 1)
        hooked(hooks, "steps")

        for p, (low, size) in enumerate(pieces[1]):
            @functools.partial(block)
            def _(p=p, low=low, size=size):
                rows_of = slice(low, low + size)
                back = []
                for c in (2, 0, 1):
                    back.append(mm(
                        beside([grads[c][n] for n in range(heads)]),
                        beside([weights[c][n, rows_of] for n in range(heads)]),
                        NT,
                    ))
                result = (back[0] + back[1] + back[2]).astype(BF16)
                part[1, t, :, :, pl.ds(low, size)] = result.reshape(
                    part.shape[2:4] + (size,)
                )
                begin(1, t, p)
            hooked(hooks, f"back{p}")

    def tables(low, high):
        def run(b, carry):
            chosen = buckets[...] == b
            sums[b] = jnp.concatenate(
                [
                    jnp.sum(jnp.where(chosen, total[h], 0.0), axis=0, keepdims=True)
                    for h in range(total.shape[0])
                ],
                axis=0,
            )
            return carry

        lax.fori_loop(low, high, run, 0)

    def fetch_out(b):
        return pltpu.make_async_copy(
            wo_hbm.at[:, pl.ds(b * lanes, lanes)], wo.at[b], wo_sem.at[b]
        )

    small = [
        pltpu.make_async_copy(source, target, in_sem.at[n])
        for n, (source, target) in enumerate((
            (labels_hbm, labels), (buckets_hbm, buckets), (gain_hbm, gain),
            (rising, cur.at[0, 0]), (falling, cur.at[1, 0]),
            (stash_hbm, stash), (queue_hbm, queue),
        ))
    ]
    for copy in small[:-1]:
        copy.start()
    fetch(0).start()
    small[-1].start()
    fetch(1).start()
    barrier = pltpu.get_barrier_semaphore()
    greeted = [twin] + [peer(k) * 2 + core for k in range(1, chips)]
    for other in greeted:
        pl.semaphore_signal(barrier, inc=1, device_id={"head": other}, device_id_type=MESH)

    @pl.when(section > 0)
    def _():
        pl.semaphore_signal(
            barrier, inc=1, device_id={"section": section - 1}, device_id_type=MESH
        )

    @pl.when(section < sections - 1)
    def _():
        pl.semaphore_signal(
            barrier, inc=1, device_id={"section": section + 1}, device_id_type=MESH
        )

    small[0].wait()
    small[1].wait()
    blank = jnp.zeros((heads, lanes - labels.shape[1]), F32)
    lookup = jnp.concatenate([labels[...], blank], axis=1)
    for n in range(heads):
        bias[n] = jnp.take_along_axis(
            jnp.broadcast_to(lookup[n : n + 1], (rows, lanes)), buckets[...], axis=1
        )
    for copy in small[2:]:
        copy.wait()
    lower(flat(cur[1, 0]))
    normalize(0, flat(cur[0, 0]))
    for t in range(ticks):
        normalize(t + 1, flat(stash[t]))

    blocks = width // group
    fetch(0).wait()

    def first(n, carry):
        relay_weights(0, n * 4, 4)
        return carry

    lax.fori_loop(0, blocks // 4, first, 0)
    fetch(2).start()
    for b in range(tiles):
        fetch_out(b).start()

    for c in (1, 2):
        fetch(c).wait()

        stride = 2 if steps % 2 == 0 else 1

        def under(turn, carry, c=c):
            for n in range(stride):
                step = turn * stride + n
                project(c - 1, step, 0, 2)
                relay_weights(c, step * (blocks // steps), blocks // steps)
            return carry

        lax.fori_loop(0, steps // stride, under, 0)
    for b in range(tiles):
        fetch_out(b).wait()
    pl.semaphore_wait(
        barrier,
        len(greeted)
        + (section > 0).astype(jnp.int32)
        + (section < sections - 1).astype(jnp.int32),
    )

    def do(function, *args):
        return lambda: function(*args)

    def both(function, which, t):
        return [do(function, which, t, j) for j in range(halves)]

    forward(0, {}, also=1)
    for t in range(ticks):
        down = range(len(pieces[1]))
        backward(t, {
            0: both(fold, 0, t),
            "steps": [do(finish_up, t, 0)],
            "back0": [do(finish_up, t, j) for j in range(1, halves)],
            f"back{down[-2]}": [do(fold, 1, t, p) for p in down[:-2]],
            f"back{down[-1]}": [do(fold, 1, t, p) for p in down[-2:-1]] + [do(relay, 0, t, 0)],
        })
        if t < last:
            final = do(fold, 1, t, down[-1])
            others = [do(relay, 0, t, j) for j in range(1, halves)]
            middle = min(1, steps - 1)
            fill(t + 2, {
                "mid": [final], "pairs": others, max(steps - 2, 0): [do(finish_down, t)],
            })
            settle(0, t)
            normalize(0, flat(cur[0, t + 1]))
            forward(t + 1, {
                "pairs": [do(relay, 1, t, 0)],
                middle: [do(relay, 1, t, j) for j in range(1, halves)],
            })
            settle(1, t)
            lower(flat(cur[1, t + 1]))
    count = sums.shape[0]
    tables(0, count // 5)
    fold(1, last, len(pieces[1]) - 1)
    for j in range(1, halves):
        relay(0, last, j)
    tables(count // 5, count * 3 // 5)
    settle(0, last)
    moved[0] = cur[0, ticks]
    finish_down(last)
    for j in range(halves):
        relay(1, last, j)
    tables(count * 3 // 5, count)
    table[...] = jnp.sum(sums[...], axis=-1)
    settle(1, last)
    moved[1] = cur[1, ticks]


def per_device(rising, falling, stash, queue, order, buckets, bias_table, gain, w_qkv, w_out):
    sections = lax.axis_size("section")
    head_count = lax.axis_size("head")
    ticks = stash.shape[1]
    rows, width = rising.shape[1:]
    heads, head_dim = w_qkv.shape[2], w_qkv.shape[4]
    chips = head_count // 2
    pair = next(p for p in (4, 2, 1) if heads % p == 0)
    others = max(chips - 1, 1)
    halves, group, lanes = 2, 16, 128
    half, quarter = width // 2, width // 4
    pieces = (
        ((0, half), (half, half)),
        ((0, half), (half, quarter), (half + quarter, quarter)),
    )
    flat_heads = heads * head_dim
    w_in = jnp.swapaxes(w_qkv[0], 1, 2)
    w_back = w_out[0].reshape(flat_heads, width)
    split = lambda a: a.reshape(a.shape[:-2] + (2, rows // 2, width))
    vmem = pl.BlockSpec(memory_space=pltpu.VMEM)
    tile = (rows // 2, width)
    bf16 = lambda *shape: pltpu.VMEM(shape, BF16)
    f32 = lambda *shape: pltpu.VMEM(shape, F32)
    dma = lambda *shape: pltpu.SemaphoreType.DMA(shape)
    moved, table = pl.pallas_call(
        functools.partial(
            wave_kernel, ticks, pair, head_dim, chips, sections, halves, pieces, group
        ),
        in_specs=[pl.BlockSpec(memory_space=pltpu.SMEM)] + [pl.BlockSpec(memory_space=pltpu.HBM)] * 9,
        out_specs=[vmem] * 2,
        out_shape=[
            jax.ShapeDtypeStruct((2, 2) + tile, BF16),
            jax.ShapeDtypeStruct((bias_table.shape[1], heads), F32),
        ],
        scratch_shapes=[
            bf16(ticks, 2, *tile),
            bf16(queue.shape[0], 2, *tile),
            f32(1, width),
            f32(heads, bias_table.shape[1]),
            pltpu.VMEM(buckets.shape, jnp.int32),
            dma(7),
            f32(heads, rows, rows),
            bf16(2, width, heads, head_dim),
            dma(3),
            bf16(width // lanes, flat_heads, lanes),
            dma(width // lanes),
            bf16(heads, width, head_dim),
            bf16(heads, width, head_dim),
            bf16(heads, width, head_dim),
            bf16(heads, (ticks + 1) * rows, head_dim),
            bf16(heads, (ticks + 1) * rows, head_dim),
            bf16(heads, (ticks + 1) * rows, head_dim),
            bf16(width // lanes, (ticks + 1) * rows, lanes),
            f32(heads, rows, rows),
            bf16(heads, rows, head_dim),
            bf16(heads, rows, head_dim),
            bf16(heads, rows, head_dim),
            bf16(heads, rows, head_dim),
            bf16(heads, rows, head_dim),
            bf16(2, pair, rows, rows),
            bf16(width // lanes, rows, lanes),
            f32(heads, rows, rows),
            f32(bias_table.shape[1], heads, rows),
            bf16(2, ticks + 1, 2, *tile),
            bf16(2, ticks, 2, *tile),
            bf16(2, ticks, *tile),
            bf16(2, ticks, chips, *tile),
            bf16(2, ticks, *tile),
            dma(2, ticks, 3), dma(2, ticks, 3),
            dma(2, ticks, 3, others), dma(2, ticks, 3, others),
            dma(2, ticks, halves), dma(2, ticks, halves),
            dma(2, ticks, halves), dma(2, ticks, halves),
        ],
        compiler_params=pltpu.CompilerParams(
            collective_id=0, has_side_effects=True, vmem_limit_bytes=54 << 20
        ),
    )(
        order, split(rising[0]), split(falling[0]), split(stash[0]), split(queue), gain,
        bias_table[0].T, buckets, w_in, w_back,
    )
    moved = moved.reshape(2, 1, rows, width)
    return (moved[0], moved[1], table[None])


def solution(mesh):
    return jax.shard_map(
        per_device,
        mesh=mesh,
        in_specs=(
            P(("groups", "section"), None, None),
            P(("groups", "section"), None, None),
            P(("groups", "section"), None, None, None),
            P("groups", None, None),
            P("groups"),
            P(),
            P("section", None, "head"),
            P("section", None),
            P("section", None, "head", None, None),
            P("section", "head", None, None),
        ),
        out_specs=(
            P(("groups", "section"), None, None),
            P(("groups", "section"), None, None),
            P(("groups", "section"), None, "head"),
        ),
        check_vma=False,
    )
```

```python
import functools

import jax
import jax.numpy as jnp
from jax import lax
from jax.experimental import pallas as pl
from jax.experimental.pallas import tpu as pltpu
from jax.sharding import PartitionSpec as P

EPSILON = 1e-06
MESH = pl.DeviceIdType.MESH
NN = (((1,), (0,)), ((), ()))
NT = (((1,), (1,)), ((), ()))
TN = (((0,), (0,)), ((), ()))
BF16 = jnp.bfloat16
F32 = jnp.float32


def mm(a, b, dims):
    return lax.dot_general(a, b, dims, preferred_element_type=F32)


def inverse_rms(x):
    return lax.rsqrt(jnp.mean(x * x, axis=-1, keepdims=True) + EPSILON)


def softmax(scores):
    raised = jnp.exp(scores - jnp.max(scores, axis=-1, keepdims=True))
    return raised * (1.0 / jnp.sum(raised, axis=-1, keepdims=True))


def wave_kernel(
    ticks, pair, head_dim, chips, sections, halves, pieces, group,
    order, rising, falling, stash_hbm, queue_hbm, gain_hbm, labels_hbm, buckets_hbm,
    w_hbm, wo_hbm,
    moved, table,
    stash, queue, gain, labels, buckets, in_sem,
    bias, raw, w_sem, wo, wo_sem, wq, wk, wv, aq, ak, av, normed, probs, attended,
    gflat, gq, gk, gv, thin, flat_down, total, sums,
    cur, part, near, far, share,
    near_send, near_recv, far_send, far_recv,
    lift_send, lift_recv, pass_send, pass_recv,
):
    section = lax.axis_index("section")
    head = lax.axis_index("head")
    chip, core = head // 2, lax.rem(head, 2)
    twin = chip * 2 + (1 - core)
    heads, rows = total.shape[:2]
    lanes = flat_down.shape[2]
    tiles = flat_down.shape[0]
    width = tiles * lanes
    steps = heads // pair
    scale = head_dim ** (-0.5)
    half = width // halves
    weights, acts, grads = (wq, wk, wv), (aq, ak, av), (gq, gk, gv)
    last = ticks - 1

    def peer(k):
        return lax.rem(chip + k, chips)

    def remote(src, dst, send, recv, target):
        return pltpu.make_async_remote_copy(
            src_ref=src, dst_ref=dst, send_sem=send, recv_sem=recv,
            device_id=target, device_id_type=MESH,
        )

    def flat(x):
        return x.astype(F32).reshape(rows, width)

    def cut(j):
        return pl.ds(j * half, half)

    def piece(which, p):
        return pl.ds(pieces[which][p][0], pieces[which][p][1])

    def near_copy(which, t, p):
        return remote(
            part.at[which, t, 1 - core, :, piece(which, p)],
            near.at[which, t, :, piece(which, p)],
            near_send.at[which, t, p], near_recv.at[which, t, p], {"head": twin},
        )

    def far_copy(which, t, p, k):
        rows_here = far.at[which, t, chip, :, piece(which, p)]
        return remote(
            rows_here, rows_here,
            far_send.at[which, t, p, k - 1], far_recv.at[which, t, p, k - 1],
            {"head": peer(k) * 2 + core},
        )

    def lift_copy(which, t, j, target):
        return remote(
            share.at[which, t, :, cut(j)], cur.at[which, t + 1, core, :, cut(j)],
            lift_send.at[which, t, j], lift_recv.at[which, t, j], {"section": target},
        )

    def pass_copy(which, t, j):
        rows_here = cur.at[which, t + 1, core, :, cut(j)]
        return remote(
            rows_here, rows_here,
            pass_send.at[which, t, j], pass_recv.at[which, t, j], {"head": twin},
        )

    def begin(which, t, p):
        near_copy(which, t, p).start()

    def fold(which, t, p):
        near_copy(which, t, p).wait_recv()
        far[which, t, chip, :, piece(which, p)] = (
            part[which, t, core, :, piece(which, p)].astype(F32)
            + near[which, t, :, piece(which, p)].astype(F32)
        ).astype(BF16)
        for k in range(1, chips):
            far_copy(which, t, p, k).start()

    def ends(which):
        if which == 0:
            return section < sections - 1, section + 1, section > 0, section - 1
        return section > 0, section - 1, section < sections - 1, section + 1

    def reduced(which, t, p):
        for k in range(1, chips):
            far_copy(which, t, p, k).wait_recv()
        own = far[which, t, 0, :, piece(which, p)].astype(F32)
        for c in range(1, chips):
            own = own + far[which, t, c, :, piece(which, p)].astype(F32)
        return own

    def hand_on(which, t, j, result):
        sends, target, receives, _ = ends(which)
        if t == last:
            cur[which, t + 1, core, :, cut(j)] = result
            return
        share[which, t, :, cut(j)] = result

        @pl.when(sends)
        def _():
            lift_copy(which, t, j, target).start()

        @pl.when(jnp.logical_not(receives))
        def _():
            if which == 0:
                cur[which, t + 1, core, :, cut(j)] = queue[order[t], core, :, cut(j)]
            else:
                cur[which, t + 1, core, :, cut(j)] = share[0, t, :, cut(j)]

    def finish_up(t, j):
        before = cur[0, t, core, :, cut(j)].astype(F32)
        hand_on(0, t, j, (before + reduced(0, t, j)).astype(BF16))

    def finish_down(t):
        own = jnp.concatenate([reduced(1, t, p) for p in range(len(pieces[1]))], axis=-1)
        before = cur[1, t, core].astype(F32)
        x = stash[t, core].astype(F32)
        inverse = inverse_rms(x)
        cubed = inverse * inverse * inverse
        weighted = gain[...] * own
        result = (
            before
            + inverse * weighted
            - x * cubed * jnp.mean(x * weighted, axis=-1, keepdims=True)
        ).astype(BF16)
        for j in range(halves):
            hand_on(1, t, j, result[:, j * half : (j + 1) * half])

    def relay(which, t, j):
        _, _, receives, source = ends(which)
        if t < last:
            @pl.when(receives)
            def _():
                lift_copy(which, t, j, source).wait_recv()

        pass_copy(which, t, j).start()

    def settle(which, t):
        sends, target, _, _ = ends(which)
        for j in range(halves):
            pass_copy(which, t, j).wait_recv()
        for p in range(len(pieces[which])):
            near_copy(which, t, p).wait_send()
            for k in range(1, chips):
                far_copy(which, t, p, k).wait_send()
        for j in range(halves):
            pass_copy(which, t, j).wait_send()
            if t < last:
                @pl.when(sends)
                def _(j=j):
                    lift_copy(which, t, j, target).wait_send()

    def beside(blocks):
        return jnp.concatenate(blocks, axis=1)

    def fetch(c):
        return pltpu.make_async_copy(w_hbm.at[:, c], raw.at[c % 2], w_sem.at[c])

    def relay_weights(c, low, count):
        for n in range(count):
            at = pl.ds(pl.multiple_of((low + n) * group, group), group)
            turned = jnp.swapaxes(raw[c % 2, at], 0, 1)
            for h in range(heads):
                weights[c][h, at] = turned[h]

    def normalize(place, x):
        y = (x * inverse_rms(x) * gain[...]).astype(BF16)
        for b in range(tiles):
            normed[b, place * rows : (place + 1) * rows] = y[:, b * lanes : (b + 1) * lanes]

    def lower(x):
        y = x.astype(BF16)
        for b in range(tiles):
            flat_down[b] = y[:, b * lanes : (b + 1) * lanes]

    def project(c, step, place, count=1):
        at = slice(place * rows, (place + count) * rows)
        result = mm(
            beside([normed[b, at] for b in range(tiles)]),
            beside([weights[c][step * pair + h] for h in range(pair)]),
            NN,
        ).astype(BF16)
        for h in range(pair):
            acts[c][step * pair + h, at] = result[:, h * head_dim : (h + 1) * head_dim]

    def project_pairs(place, hooks):
        for step in range(steps):
            if step == steps // 2:
                hooked(hooks, "mid")
            project(0, step, place)
            project(1, step, place)
        hooked(hooks, "pairs")

    def block(emit):
        pl.when(section >= 0)(emit)

    def act(c, place, n):
        return acts[c][n, place * rows : (place + 1) * rows]

    def score(place, step):
        return [
            mm(act(0, place, n), act(1, place, n), NT) * scale + bias[n]
            for n in range(step * pair, (step + 1) * pair)
        ]

    def hooked(hooks, n):
        for action in hooks.get(n, ()):
            action()

    def blend(t, step, scores):
        for h in range(pair):
            probs16 = softmax(scores[h]).astype(BF16)
            n = step * pair + h
            attended[n] = mm(probs16, act(2, 0, n), NN).astype(BF16)

    def keep(step, scores):
        for h in range(pair):
            probs[step * pair + h] = softmax(scores[h])

    def out(t):
        for j in range(halves):
            each = half // lanes
            right = beside([wo[b] for b in range(j * each, (j + 1) * each)])
            left = beside([attended[n] for n in range(heads)])
            result = mm(left, right, NN).astype(BF16)
            part[0, t, :, :, cut(j)] = result.reshape(part.shape[2:4] + (half,))
            begin(0, t, j)

    def forward(t, hooks, also=None):
        count = 1 if also is None else 2
        if also is None:
            project_pairs(0, hooks)

        @functools.partial(block)
        def _():
            scores = {n: score(0, n) for n in range(min(2, steps))}
            for step in range(steps):
                project(2, step, 0, count)
                extra = score(also, step) if also is not None else None
                if 2 <= step + 2 < steps:
                    scores[step + 2] = score(0, step + 2)
                blend(t, step, scores.pop(step))
                if extra is not None:
                    keep(step, extra)
                hooked(hooks, step)
            out(t)
        hooked(hooks, "end")

    def fill(place, hooks):
        project_pairs(place, hooks)

        @functools.partial(block)
        def _():
            scores = {n: score(place, n) for n in range(min(2, steps))}
            for step in range(steps):
                project(2, step, place)
                if step + 2 < steps:
                    scores[step + 2] = score(place, step + 2)
                keep(step, scores.pop(step))
                hooked(hooks, step)
        hooked(hooks, "end")

    def backward(t, hooks):
        place = t + 1

        def open_grad(step):
            block = slice(step * pair * head_dim, (step + 1) * pair * head_dim)
            result = mm(
                beside([flat_down[b] for b in range(tiles)]),
                beside([wo[b, block] for b in range(tiles)]),
                NT,
            ).astype(BF16)
            for h in range(pair):
                gflat[step * pair + h] = result[:, h * head_dim : (h + 1) * head_dim]

        def score_grads(step):
            for h in range(pair):
                n = step * pair + h
                g = gflat[n]
                grad_probs = mm(g, act(2, place, n), NT)
                p = probs[n]
                gv[n] = mm(p.astype(BF16), g, TN).astype(BF16)
                grad_scores = p * (
                    grad_probs - jnp.sum(p * grad_probs, axis=-1, keepdims=True)
                )
                thin[step % 2, h] = grad_scores.astype(BF16)
                if t == 0:
                    total[n] = grad_scores
                else:
                    total[n] += grad_scores

        def query_key_grads(step):
            for h in range(pair):
                n = step * pair + h
                small = thin[step % 2, h]
                gq[n] = (mm(small, act(1, place, n), NN) * scale).astype(BF16)
                gk[n] = (mm(small, act(0, place, n), TN) * scale).astype(BF16)

        @functools.partial(block)
        def _():
            open_grad(0)
            for step in range(steps):
                score_grads(step)
                if step + 1 < steps:
                    open_grad(step + 1)
                if step > 0:
                    query_key_grads(step - 1)
                hooked(hooks, step)
            query_key_grads(steps - 1)
        hooked(hooks, "steps")

        for p, (low, size) in enumerate(pieces[1]):
            @functools.partial(block)
            def _(p=p, low=low, size=size):
                rows_of = slice(low, low + size)
                back = []
                for c in (2, 0, 1):
                    back.append(mm(
                        beside([grads[c][n] for n in range(heads)]),
                        beside([weights[c][n, rows_of] for n in range(heads)]),
                        NT,
                    ))
                result = (back[0] + back[1] + back[2]).astype(BF16)
                part[1, t, :, :, pl.ds(low, size)] = result.reshape(
                    part.shape[2:4] + (size,)
                )
                begin(1, t, p)
            hooked(hooks, f"back{p}")

    def tables(low, high):
        def run(b, carry):
            chosen = buckets[...] == b
            sums[b] = jnp.concatenate(
                [
                    jnp.sum(jnp.where(chosen, total[h], 0.0), axis=0, keepdims=True)
                    for h in range(total.shape[0])
                ],
                axis=0,
            )
            return carry

        lax.fori_loop(low, high, run, 0)

    def fetch_out(b):
        return pltpu.make_async_copy(
            wo_hbm.at[:, pl.ds(b * lanes, lanes)], wo.at[b], wo_sem.at[b]
        )

    small = [
        pltpu.make_async_copy(source, target, in_sem.at[n])
        for n, (source, target) in enumerate((
            (labels_hbm, labels), (buckets_hbm, buckets), (gain_hbm, gain),
            (rising, cur.at[0, 0]), (falling, cur.at[1, 0]),
            (stash_hbm, stash), (queue_hbm, queue),
        ))
    ]
    for copy in small[:-1]:
        copy.start()
    fetch(0).start()
    small[-1].start()
    fetch(1).start()
    barrier = pltpu.get_barrier_semaphore()
    greeted = [twin] + [peer(k) * 2 + core for k in range(1, chips)]
    for other in greeted:
        pl.semaphore_signal(barrier, inc=1, device_id={"head": other}, device_id_type=MESH)

    @pl.when(section > 0)
    def _():
        pl.semaphore_signal(
            barrier, inc=1, device_id={"section": section - 1}, device_id_type=MESH
        )

    @pl.when(section < sections - 1)
    def _():
        pl.semaphore_signal(
            barrier, inc=1, device_id={"section": section + 1}, device_id_type=MESH
        )

    small[0].wait()
    small[1].wait()
    blank = jnp.zeros((heads, lanes - labels.shape[1]), F32)
    lookup = jnp.concatenate([labels[...], blank], axis=1)
    for n in range(heads):
        bias[n] = jnp.take_along_axis(
            jnp.broadcast_to(lookup[n : n + 1], (rows, lanes)), buckets[...], axis=1
        )
    for copy in small[2:]:
        copy.wait()
    lower(flat(cur[1, 0]))
    normalize(0, flat(cur[0, 0]))
    for t in range(ticks):
        normalize(t + 1, flat(stash[t]))

    blocks = width // group
    fetch(0).wait()

    def first(n, carry):
        relay_weights(0, n * 4, 4)
        return carry

    lax.fori_loop(0, blocks // 4, first, 0)
    fetch(2).start()
    for b in range(tiles):
        fetch_out(b).start()

    for c in (1, 2):
        fetch(c).wait()

        stride = 2 if steps % 2 == 0 else 1

        def under(turn, carry, c=c):
            for n in range(stride):
                step = turn * stride + n
                project(c - 1, step, 0, 2)
                relay_weights(c, step * (blocks // steps), blocks // steps)
            return carry

        lax.fori_loop(0, steps // stride, under, 0)
    for b in range(tiles):
        fetch_out(b).wait()
    pl.semaphore_wait(
        barrier,
        len(greeted)
        + (section > 0).astype(jnp.int32)
        + (section < sections - 1).astype(jnp.int32),
    )

    def do(function, *args):
        return lambda: function(*args)

    def both(function, which, t):
        return [do(function, which, t, j) for j in range(halves)]

    forward(0, {}, also=1)
    for t in range(ticks):
        down = range(len(pieces[1]))
        tail = [do(fold, 1, t, down[-2])]
        backward(t, {
            min(1, steps - 1): both(fold, 0, t),
            "back0": [do(finish_up, t, 0)],
            f"back{down[-2]}": [do(finish_up, t, j) for j in range(1, halves)]
            + [do(fold, 1, t, p) for p in down[:-2]],
            f"back{down[-1]}": tail if t == last else [],
        })
        if t < last:
            final = [do(fold, 1, t, down[-1])]
            fill(t + 2, {
                "mid": tail + final, "pairs": both(relay, 0, t), "end": [do(finish_down, t)],
            })
            settle(0, t)
            normalize(0, flat(cur[0, t + 1]))
            forward(t + 1, {steps - 1: both(relay, 1, t)})
            settle(1, t)
            lower(flat(cur[1, t + 1]))
    count = sums.shape[0]
    tables(0, count // 5)
    fold(1, last, len(pieces[1]) - 1)
    for j in range(halves):
        relay(0, last, j)
    tables(count // 5, count * 3 // 5)
    settle(0, last)
    moved[0] = cur[0, ticks]
    finish_down(last)
    for j in range(halves):
        relay(1, last, j)
    tables(count * 3 // 5, count)
    table[...] = jnp.sum(sums[...], axis=-1)
    settle(1, last)
    moved[1] = cur[1, ticks]


def per_device(rising, falling, stash, queue, order, buckets, bias_table, gain, w_qkv, w_out):
    sections = lax.axis_size("section")
    head_count = lax.axis_size("head")
    ticks = stash.shape[1]
    rows, width = rising.shape[1:]
    heads, head_dim = w_qkv.shape[2], w_qkv.shape[4]
    chips = head_count // 2
    pair = next(p for p in (4, 2, 1) if heads % p == 0)
    others = max(chips - 1, 1)
    halves, group, lanes = 2, 16, 128
    half, quarter = width // 2, width // 4
    pieces = (
        ((0, half), (half, half)),
        ((0, half), (half, quarter), (half + quarter, quarter)),
    )
    flat_heads = heads * head_dim
    w_in = jnp.swapaxes(w_qkv[0], 1, 2)
    w_back = w_out[0].reshape(flat_heads, width)
    split = lambda a: a.reshape(a.shape[:-2] + (2, rows // 2, width))
    vmem = pl.BlockSpec(memory_space=pltpu.VMEM)
    tile = (rows // 2, width)
    bf16 = lambda *shape: pltpu.VMEM(shape, BF16)
    f32 = lambda *shape: pltpu.VMEM(shape, F32)
    dma = lambda *shape: pltpu.SemaphoreType.DMA(shape)
    moved, table = pl.pallas_call(
        functools.partial(
            wave_kernel, ticks, pair, head_dim, chips, sections, halves, pieces, group
        ),
        in_specs=[pl.BlockSpec(memory_space=pltpu.SMEM)] + [pl.BlockSpec(memory_space=pltpu.HBM)] * 9,
        out_specs=[vmem] * 2,
        out_shape=[
            jax.ShapeDtypeStruct((2, 2) + tile, BF16),
            jax.ShapeDtypeStruct((bias_table.shape[1], heads), F32),
        ],
        scratch_shapes=[
            bf16(ticks, 2, *tile),
            bf16(queue.shape[0], 2, *tile),
            f32(1, width),
            f32(heads, bias_table.shape[1]),
            pltpu.VMEM(buckets.shape, jnp.int32),
            dma(7),
            f32(heads, rows, rows),
            bf16(2, width, heads, head_dim),
            dma(3),
            bf16(width // lanes, flat_heads, lanes),
            dma(width // lanes),
            bf16(heads, width, head_dim),
            bf16(heads, width, head_dim),
            bf16(heads, width, head_dim),
            bf16(heads, (ticks + 1) * rows, head_dim),
            bf16(heads, (ticks + 1) * rows, head_dim),
            bf16(heads, (ticks + 1) * rows, head_dim),
            bf16(width // lanes, (ticks + 1) * rows, lanes),
            f32(heads, rows, rows),
            bf16(heads, rows, head_dim),
            bf16(heads, rows, head_dim),
            bf16(heads, rows, head_dim),
            bf16(heads, rows, head_dim),
            bf16(heads, rows, head_dim),
            bf16(2, pair, rows, rows),
            bf16(width // lanes, rows, lanes),
            f32(heads, rows, rows),
            f32(bias_table.shape[1], heads, rows),
            bf16(2, ticks + 1, 2, *tile),
            bf16(2, ticks, 2, *tile),
            bf16(2, ticks, *tile),
            bf16(2, ticks, chips, *tile),
            bf16(2, ticks, *tile),
            dma(2, ticks, 3), dma(2, ticks, 3),
            dma(2, ticks, 3, others), dma(2, ticks, 3, others),
            dma(2, ticks, halves), dma(2, ticks, halves),
            dma(2, ticks, halves), dma(2, ticks, halves),
        ],
        compiler_params=pltpu.CompilerParams(
            collective_id=0, has_side_effects=True, vmem_limit_bytes=54 << 20
        ),
    )(
        order, split(rising[0]), split(falling[0]), split(stash[0]), split(queue), gain,
        bias_table[0].T, buckets, w_in, w_back,
    )
    moved = moved.reshape(2, 1, rows, width)
    return (moved[0], moved[1], table[None])


def solution(mesh):
    return jax.shard_map(
        per_device,
        mesh=mesh,
        in_specs=(
            P(("groups", "section"), None, None),
            P(("groups", "section"), None, None),
            P(("groups", "section"), None, None, None),
            P("groups", None, None),
            P("groups"),
            P(),
            P("section", None, "head"),
            P("section", None),
            P("section", None, "head", None, None),
            P("section", "head", None, None),
        ),
        out_specs=(
            P(("groups", "section"), None, None),
            P(("groups", "section"), None, None),
            P(("groups", "section"), None, "head"),
        ),
        check_vma=False,
    )
```
